512 devices in a mesh: tm: 16 (over x_hi, y), height: 32 (over z, x_lo, core).
Axes of the slice: x: 4 (x_hi: 2, x_lo: 2; x = x_hi * 2 + x_lo), y: 8, z: 8, core: 2. Of those that a mesh axis runs over, the one named last changes fastest.
Arguments:
- tokens: bfloat16 [16, 64, 96, 384], P('tm', 'height'), may hold values from -6 to 6
- cotangent: bfloat16 [16, 64, 96, 384], P('tm', 'height'), may hold values from -6 to 6
- key_blocks: int32 [16, 32, 3, 12], P('tm', 'height'), may hold values from 0 to 26, as said below
- qkv_weight: bfloat16 [384, 1152], replicated, as said below
- out_weight: bfloat16 [384, 384], replicated, may hold values from -0.3125 to 0.3125
- norm_gain: float32 [384], replicated, may hold values from 0.5 to 1.5
Outputs:
- layer_out: bfloat16 [16, 64, 96, 384], P('tm', 'height')
- grad_tokens: bfloat16 [16, 64, 96, 384], P('tm', 'height')
- grad_qkv: float32 [384, 1152], replicated
- grad_out: float32 [384, 384], replicated
- grad_gain: float32 [384], replicated
The draws below stay inside these ranges and needn't reach their ends.
Inputs may be any that keep to these rules, and one draw needn't show every extreme that they name: `key_blocks`: each list holds 12 different entries: the query block itself, the block of the same index in the tiles one frame group before and after in the same strip where those tiles exist, and others; every named block lies inside the grid and in the query's own clip, the 16 tile columns along tm forming 1 clips of equal length. `qkv_weight`: columns hold queries, keys and values in that order, each head by head.
All inputs are finite; a program needn't handle non-finite values.
Results may differ from the reference program's by a relative error of at most 0.0086.
Values may be sent and summed in bfloat16 or wider, within the bound.
A program may use at most 64 MiB of HBM per device.

```python
import math
import jax
import jax.numpy as jnp
from jax import lax

HEADS = 6
HDIM = 64
D = 384
F_DEV = 1
R_DEV = 2
WCOLS = 96
KB = 12
CLIPS = 1
NBLK = 3
FRAMES = 16
HROWS = 64
TOKENS = 98304
N_TM = 16
N_HEIGHT = 32


def draw_key_blocks(key, part):
    candidate_count = 9 * NBLK
    candidate = jnp.arange(candidate_count, dtype=jnp.int32)
    offset_time = candidate // (3 * NBLK) - 1
    offset_height = candidate // NBLK % 3 - 1
    target_block = candidate % NBLK
    time_index = jnp.arange(N_TM, dtype=jnp.int32)[:, None, None, None]
    height_index = jnp.arange(N_HEIGHT, dtype=jnp.int32)[None, :, None, None]
    query_block = jnp.arange(NBLK, dtype=jnp.int32)[None, None, :, None]
    group_length = N_TM // CLIPS
    other_time = time_index + offset_time
    other_height = height_index + offset_height
    inside = (other_time >= 0) & (other_time < N_TM) & (other_height >= 0) & (other_height < N_HEIGHT)
    same_clip = jnp.maximum(other_time, 0) // group_length == time_index // group_length
    own_block = (offset_time == 0) & (offset_height == 0) & (target_block == query_block)
    time_pair = (offset_time != 0) & (offset_height == 0) & (target_block == query_block) & inside & same_clip
    random_part = jax.random.randint(jax.random.fold_in(key, 1), (N_TM, N_HEIGHT, NBLK, candidate_count), 0, 262144)
    ranking = random_part * 4096 + candidate
    ranking = jnp.where(inside & same_clip, ranking, -1 - candidate)
    ranking = jnp.where(time_pair, 1073741823 - candidate, ranking)
    ranking = jnp.where(own_block, 1073741824, ranking)
    ignored, picked = lax.top_k(ranking, KB)
    order_scores = jax.random.randint(jax.random.fold_in(key, 2), (N_TM, N_HEIGHT, NBLK, KB), 0, 262144) * 64
    order_scores = order_scores + jnp.arange(KB, dtype=jnp.int32)
    order = jnp.argsort(order_scores, axis=-1, stable=True)
    return jnp.take_along_axis(picked, order, axis=-1).astype(jnp.int32)


def draw_qkv_weight(key, part):
    model_width = HEADS * HDIM
    base = jax.random.normal(key, (model_width, 3 * model_width), jnp.float32) / math.sqrt(model_width)
    return base.astype(jnp.bfloat16)


def levels(rng, extent, pieces, least, largest):
    level, own = 1.0, jax.random.fold_in(rng, 6)
    for dim, shards_of in pieces:
        heights = jnp.exp(jax.random.uniform(jax.random.fold_in(own, dim), (shards_of,), jnp.float32, least / len(pieces), largest / len(pieces)))
        level = level * jnp.repeat(heights, extent[dim] // shards_of).reshape([-1 if axis == dim else 1 for axis in range(len(extent))])
    return level


def noise(stream_key, extent, deviation, most, cuts=(), kind=jnp.bfloat16):
    factor_of = levels(stream_key, extent, cuts, -0.22, 0.18) if cuts else 1.0
    result = jax.random.normal(stream_key, extent, jnp.float32) * deviation * factor_of
    return jnp.minimum(jnp.maximum(result, -most), most).astype(kind)


def setup_inputs(seed: int = 0) -> dict:
    key_of = jax.random.split(jax.random.key(seed), 7)
    return {
        "tokens": noise(key_of[0], (FRAMES, HROWS, WCOLS, D), 1.0, 6.0, ((0, 16), (1, 32))),
        "cotangent": noise(key_of[1], (FRAMES, HROWS, WCOLS, D), 1.0, 6.0, ((0, 16), (1, 32))),
        "key_blocks": draw_key_blocks(jax.random.fold_in(key_of[6], 71), 0),
        "qkv_weight": draw_qkv_weight(jax.random.fold_in(key_of[6], 71), 0),
        "out_weight": noise(key_of[4], (D, D), D ** -0.5, 0.3125),
        "norm_gain": jnp.clip(jax.random.uniform(key_of[5], (D,), jnp.float32, 0.5, 1.5), 0.5, 1.5),
    }


EPSILON = 1e-05
HIGH = lax.Precision.HIGHEST

def to_tiles(tensor):
    channels = tensor.shape[-1]
    grouped = tensor.reshape(N_TM, F_DEV, N_HEIGHT, R_DEV, WCOLS, channels).transpose(0, 2, 1, 3, 4, 5)
    return grouped.reshape(N_TM, N_HEIGHT, F_DEV * R_DEV * WCOLS, channels)

def from_tiles(tensor):
    channels = tensor.shape[-1]
    grouped = tensor.reshape(N_TM, N_HEIGHT, F_DEV, R_DEV, WCOLS, channels).transpose(0, 2, 1, 3, 4, 5)
    return grouped.reshape(N_TM * F_DEV, N_HEIGHT * R_DEV, WCOLS, channels)

def normalize(token_rows, norm_gain):
    values_in = token_rows.astype(jnp.float32)
    center = lax.optimization_barrier(jnp.mean(values_in, -1, keepdims=True))
    spread = lax.optimization_barrier(jnp.mean(jnp.square(values_in - center), -1, keepdims=True))
    inverse_scale = lax.rsqrt(spread + EPSILON)
    centred = (values_in - center) * inverse_scale
    normed = (centred * norm_gain).astype(jnp.bfloat16)
    return (values_in, centred, normed, inverse_scale)

def local_attention(queries, neighbourhood, block_list, grad_attended):
    token_count, model_width = queries.shape
    block_count, list_length = block_list.shape
    block_rows = token_count // block_count
    head_dim = model_width // HEADS
    score_scale = 1.0 / math.sqrt(head_dim)
    chosen = jnp.take(neighbourhood.reshape(-1, block_rows, 2 * model_width), block_list.reshape(-1), axis=0)
    chosen = chosen.reshape(block_count, list_length * block_rows, 2 * model_width).astype(jnp.float32)
    key_heads = chosen[..., :model_width].reshape(block_count, list_length * block_rows, HEADS, head_dim)
    value_heads = chosen[..., model_width:].reshape(block_count, list_length * block_rows, HEADS, head_dim)
    query_heads = queries.astype(jnp.float32).reshape(block_count, block_rows, HEADS, head_dim)
    scores = jnp.einsum('nqhd,nkhd->nhqk', query_heads, key_heads, precision=HIGH) * score_scale
    row_max = lax.optimization_barrier(jnp.max(scores, -1, keepdims=True))
    raw_weights = jnp.exp(scores - row_max)
    weights_full = raw_weights / lax.optimization_barrier(jnp.sum(raw_weights, -1, keepdims=True))
    weights_low = weights_full.astype(jnp.bfloat16).astype(jnp.float32)
    attended = jnp.einsum('nhqk,nkhd->nqhd', weights_low, value_heads, precision=HIGH)
    attended = attended.astype(jnp.bfloat16).reshape(token_count, model_width)
    grad_heads = grad_attended.astype(jnp.float32).reshape(block_count, block_rows, HEADS, head_dim)
    grad_probs = jnp.einsum('nqhd,nkhd->nhqk', grad_heads, value_heads, precision=HIGH)
    row_dots = lax.optimization_barrier(jnp.sum(weights_full * grad_probs, -1, keepdims=True))
    grad_scores = (weights_full * (grad_probs - row_dots) * score_scale).astype(jnp.bfloat16).astype(jnp.float32)
    grad_queries = jnp.einsum('nhqk,nkhd->nqhd', grad_scores, key_heads, precision=HIGH)
    grad_queries = grad_queries.astype(jnp.bfloat16).reshape(token_count, model_width)
    grad_keys = jnp.einsum('nhqk,nqhd->nkhd', grad_scores, query_heads, precision=HIGH)
    grad_values = jnp.einsum('nhqk,nqhd->nkhd', weights_low, grad_heads, precision=HIGH)
    grad_pairs = jnp.concatenate([grad_keys.reshape(block_count * list_length, block_rows, model_width), grad_values.reshape(block_count * list_length, block_rows, model_width)], axis=-1)
    grad_pairs = grad_pairs.reshape(block_count * list_length, block_rows * 2 * model_width)
    selector = (block_list.reshape(1, -1) == jnp.arange(9 * block_count, dtype=jnp.int32)[:, None]).astype(jnp.float32)
    key_terms = jnp.dot(selector, grad_pairs, precision=HIGH)
    key_terms = key_terms.reshape(9 * token_count, 2 * model_width).astype(jnp.bfloat16)
    return (attended, grad_queries, key_terms)

def reference(tokens, cotangent, key_blocks, qkv_weight, out_weight, norm_gain):
    model_width = tokens.shape[-1]
    token_count = F_DEV * R_DEV * WCOLS
    token_rows = to_tiles(tokens).reshape(-1, model_width)
    values_in, centred, normed, inverse_scale = normalize(token_rows, norm_gain)
    projected = jnp.dot(normed, qkv_weight, preferred_element_type=jnp.float32).astype(jnp.bfloat16)
    queries = projected[:, :model_width].reshape(N_TM, N_HEIGHT, token_count, model_width)
    keyvals = projected[:, model_width:].reshape(N_TM, N_HEIGHT, token_count, 2 * model_width)
    padded = jnp.pad(keyvals, ((1, 1), (1, 1), (0, 0), (0, 0)))
    grad_rows_out = to_tiles(cotangent).reshape(-1, model_width)
    grad_attended = lax.dot_general(grad_rows_out, out_weight, (((1,), (1,)), ((), ())), preferred_element_type=jnp.float32).astype(jnp.bfloat16)
    grad_tiles = grad_attended.reshape(N_TM, N_HEIGHT, token_count, model_width)
    zero_index = jnp.zeros((), jnp.int32)

    def visit(accumulated, device_index):
        time_index = (device_index // N_HEIGHT).astype(jnp.int32)
        height_index = (device_index % N_HEIGHT).astype(jnp.int32)
        neighbourhood = lax.dynamic_slice(padded, (time_index, height_index, zero_index, zero_index), (3, 3, token_count, 2 * model_width))
        neighbourhood = neighbourhood.reshape(9 * token_count, 2 * model_width)
        attended, grad_queries, key_terms = local_attention(queries[time_index, height_index], neighbourhood, key_blocks[time_index, height_index], grad_tiles[time_index, height_index])
        current = lax.dynamic_slice(accumulated, (time_index, height_index, zero_index, zero_index), (3, 3, token_count, 2 * model_width))
        current = current + key_terms.reshape(3, 3, token_count, 2 * model_width).astype(accumulated.dtype)
        accumulated = lax.dynamic_update_slice(accumulated, current, (time_index, height_index, zero_index, zero_index))
        return (accumulated, (attended, grad_queries))
    zero_grid = jnp.zeros((N_TM + 2, N_HEIGHT + 2, token_count, 2 * model_width), jnp.float32)
    totals, (attended, grad_queries) = lax.scan(visit, zero_grid, jnp.arange(N_TM * N_HEIGHT, dtype=jnp.int32))
    grad_keyvals = totals[1:-1, 1:-1].astype(jnp.bfloat16).reshape(-1, 2 * model_width)
    attended = attended.reshape(-1, model_width)
    grad_queries = grad_queries.reshape(-1, model_width)
    layer_rows = (values_in + jnp.dot(attended, out_weight, preferred_element_type=jnp.float32)).astype(jnp.bfloat16)
    grad_rows = jnp.concatenate([grad_queries, grad_keyvals], axis=1)
    factor = 1.0 / math.sqrt(TOKENS)
    grad_qkv = lax.dot_general(normed, grad_rows, (((0,), (0,)), ((), ())), preferred_element_type=jnp.float32) * factor
    grad_out = lax.dot_general(attended, grad_rows_out, (((0,), (0,)), ((), ())), preferred_element_type=jnp.float32) * factor
    grad_normed = lax.dot_general(grad_rows, qkv_weight, (((1,), (1,)), ((), ())), preferred_element_type=jnp.float32)
    grad_gain = lax.optimization_barrier(jnp.sum(grad_normed * centred, 0)) * factor
    scaled = grad_normed * norm_gain
    grad_inner = inverse_scale * (scaled - lax.optimization_barrier(jnp.mean(scaled, -1, keepdims=True)) - centred * lax.optimization_barrier(jnp.mean(scaled * centred, -1, keepdims=True)))
    grad_tokens = (grad_rows_out.astype(jnp.float32) + grad_inner).astype(jnp.bfloat16)
    layer_tiles = layer_rows.reshape(N_TM, N_HEIGHT, token_count, model_width)
    grad_token_tiles = grad_tokens.reshape(N_TM, N_HEIGHT, token_count, model_width)
    return (from_tiles(layer_tiles), from_tiles(grad_token_tiles), grad_qkv, grad_out, grad_gain)
```

```python
import math

import jax
import jax.numpy as jnp
from jax import lax
from jax.experimental import pallas as pl
from jax.experimental.pallas import tpu as pltpu
from jax.sharding import PartitionSpec as P

HEADS = 6
EPSILON = 1e-05
F32 = jnp.float32
BF16 = jnp.bfloat16
MESH = pl.DeviceIdType.MESH
UNIT = 80


def extended(block, sides, width):
    for axis, dim in sides:
        count = lax.axis_size(axis)
        forward = [(i, i + 1) for i in range(count - 1)]
        backward = [(target, source) for source, target in forward]
        low = lax.ppermute(
            lax.slice_in_dim(block, block.shape[dim] - width, None, axis=dim), axis, forward
        )
        high = lax.ppermute(lax.slice_in_dim(block, 0, width, axis=dim), axis, backward)
        block = jnp.concatenate([low, block, high], axis=dim)
    return block


def shifted(shard, axis, by):
    size = lax.axis_size(axis)
    pairs = [(i, i + by) for i in range(size) if 0 <= i + by < size]
    return lax.ppermute(shard, axis, pairs)


def norm_parts(token_rows):
    values_in = token_rows.astype(F32)
    center = jnp.mean(values_in, -1, keepdims=True)
    spread = jnp.mean(jnp.square(values_in - center), -1, keepdims=True)
    inverse_scale = lax.rsqrt(spread + EPSILON)
    centred = (values_in - center) * inverse_scale
    return values_in, centred, inverse_scale


def dot_general(a, b, ca, cb):
    return lax.dot_general(a, b, (((ca,), (cb,)), ((), ())), preferred_element_type=F32)


def attention_kernel(list_ref, q_ref, ga_ref, nb_ref, tok_ref, ow_ref,
                     att_ref, gq_ref, terms_ref, lo_ref, acc, kv):
    blocks, length = list_ref.shape
    rows = nb_ref.shape[1]
    width = q_ref.shape[1]
    scale = 1.0 / math.sqrt(width // HEADS)
    acc[...] = jnp.zeros_like(acc)
    first = lax.broadcasted_iota(jnp.int32, (rows, 128), 1) < 64
    zero = jnp.zeros((rows, 128), BF16)

    def split(pair):
        return jnp.concatenate([jnp.where(first, pair, zero), jnp.where(first, zero, pair)], 0)

    def join(both):
        return jnp.where(first, both[:rows], both[rows:])

    def body(n, carry):
        at = pl.multiple_of(n * rows, rows)
        for j in range(length):
            kv[j * rows:(j + 1) * rows, :] = nb_ref[list_ref[n, j]]
        for p in range(width // 128):
            lanes = slice(p * 128, (p + 1) * 128)
            vlanes = slice(width + p * 128, width + (p + 1) * 128)
            qs = split(q_ref[pl.ds(at, rows), lanes])
            gs = split(ga_ref[pl.ds(at, rows), lanes])
            keys = kv[:, lanes]
            values = kv[:, vlanes]
            scores = dot_general(keys, qs, 1, 1) * scale
            top = jnp.max(scores, 0, keepdims=True)
            raw = jnp.exp(scores - top)
            full = raw / jnp.sum(raw, 0, keepdims=True)
            low = full.astype(BF16)
            att_ref[pl.ds(at, rows), lanes] = join(dot_general(low, values, 0, 0)).astype(BF16)
            probs = dot_general(values, gs, 1, 1)
            dots = jnp.sum(full * probs, 0, keepdims=True)
            grad = (full * (probs - dots) * scale).astype(BF16)
            gq_ref[pl.ds(at, rows), lanes] = join(dot_general(grad, keys, 0, 0)).astype(BF16)
            gk = dot_general(grad, qs, 1, 0)
            gv = dot_general(low, gs, 1, 0)
            for j in range(length):
                b = list_ref[n, j]
                part = slice(j * rows, (j + 1) * rows)
                acc[b, :, lanes] = acc[b, :, lanes] + gk[part]
                acc[b, :, vlanes] = acc[b, :, vlanes] + gv[part]
        return carry

    lax.fori_loop(0, blocks, body, 0)
    terms_ref[...] = acc[...].astype(BF16)
    out = dot_general(att_ref[...], ow_ref[...], 1, 0)
    lo_ref[...] = (tok_ref[...].astype(F32) + out).astype(BF16)


def attention(block_list, queries, grad_attended, neighbourhood, tokens, out_weight):
    count, width = queries.shape
    blocks = block_list.shape[0]
    rows = count // blocks
    vmem = pl.BlockSpec(memory_space=pltpu.VMEM)
    return pl.pallas_call(
        attention_kernel,
        out_shape=(
            jax.ShapeDtypeStruct((count, width), BF16),
            jax.ShapeDtypeStruct((count, width), BF16),
            jax.ShapeDtypeStruct((9 * blocks, rows, 2 * width), BF16),
            jax.ShapeDtypeStruct((count, width), BF16),
        ),
        in_specs=[pl.BlockSpec(memory_space=pltpu.SMEM)] + [vmem] * 5,
        out_specs=(vmem,) * 4,
        scratch_shapes=[
            pltpu.VMEM((9 * blocks, rows, 2 * width), F32),
            pltpu.VMEM((block_list.shape[1] * rows, 2 * width), BF16),
        ],
        compiler_params=pltpu.CompilerParams(vmem_limit_bytes=48 << 20),
        name="sparse_attention",
    )(block_list, queries, grad_attended, neighbourhood, tokens, out_weight)


def place():
    t = lax.axis_index("tm")
    h = lax.axis_index("height")
    return t // 8, lax.rem(t, 8), h // 4, lax.rem(h // 2, 2), lax.rem(h, 2)


def device(x, y, z, core):
    return ((x // 2) * 8 + y, z * 4 + lax.rem(x, 2) * 2 + core)


def reduce_kernel(factor, tok_ref, cot_ref, gain_ref, w_ref, gq_ref, gkv_ref, att_ref,
                  gt_ref, oq_ref, oo_ref, og_ref,
                  mine, rc, s1, r1, s2, r2, s3, r3, full, small, ssem, rsem):
    width = tok_ref.shape[1]
    half = 32 * UNIT
    x_hi, y, z, x_lo, core = place()
    x = x_hi * 2 + x_lo
    p = jnp.where(core == 0, z, y)
    q = jnp.where(core == 0, y, z)

    def on_core():
        return device(x, y, z, 1 - core)

    def on_x(d):
        return device(lax.rem(x + d, 4), y, z, core)

    def on_first(d):
        there = lax.rem(p + d, 8)
        return device(x, jnp.where(core == 0, y, there), jnp.where(core == 0, there, z), core)

    def on_second(d):
        there = lax.rem(q + d, 8)
        return device(x, jnp.where(core == 0, there, y), jnp.where(core == 0, z, there), core)

    def send(src, dst, slot, target):
        copy = pltpu.make_async_remote_copy(
            src_ref=src, dst_ref=dst, send_sem=ssem.at[slot], recv_sem=rsem.at[slot],
            device_id=target, device_id_type=MESH,
        )
        copy.start()
        return copy

    barrier = pltpu.get_barrier_semaphore()
    pl.semaphore_signal(barrier, inc=1, device_id=on_core(), device_id_type=MESH)
    for d in range(1, 4):
        pl.semaphore_signal(barrier, inc=1, device_id=on_x(d), device_id_type=MESH)
    for d in range(1, 8):
        pl.semaphore_signal(barrier, inc=1, device_id=on_first(d), device_id_type=MESH)
        pl.semaphore_signal(barrier, inc=1, device_id=on_second(d), device_id_type=MESH)

    _, centred, inverse = norm_parts(tok_ref[...])
    gain = gain_ref[...]
    normed_t = (centred * gain).astype(BF16).T
    grad_normed = dot_general(gq_ref[...], w_ref[:, :width], 1, 1)
    grad_normed += dot_general(gkv_ref[...], w_ref[:, width:], 1, 1)
    for c in range(3 * width // 128):
        if c * 128 < width:
            rhs = gq_ref[:, c * 128:(c + 1) * 128]
        else:
            rhs = gkv_ref[:, c * 128 - width:(c + 1) * 128 - width]
        mine[c * width:(c + 1) * width, :] = dot_general(normed_t, rhs, 1, 0).astype(BF16)
    att_t = att_ref[...].T
    done = 3 * width // 128 * width
    for c in range(width // 128):
        rhs = cot_ref[:, c * 128:(c + 1) * 128]
        mine[done + c * width:done + (c + 1) * width, :] = dot_general(att_t, rhs, 1, 0).astype(BF16)
    done += width // 128 * width
    local_gain = jnp.sum(grad_normed * centred, 0, keepdims=True)
    small[...] = jnp.zeros_like(small)
    for c in range(width // 128):
        small[c:c + 1, :] = local_gain[:, c * 128:(c + 1) * 128]
    mine[done:done + 16, :] = small[...].astype(BF16)
    mine[done + 16:, :] = jnp.zeros((2 * half - done - 16, 128), BF16)

    pl.semaphore_wait(barrier, 18)
    own = pl.multiple_of(core * half, half)
    other = pl.multiple_of((1 - core) * half, half)
    copy = send(mine.at[pl.ds(other, half)], rc, 0, on_core())
    scaled = grad_normed * gain
    inner = inverse * (
        scaled
        - jnp.mean(scaled, -1, keepdims=True)
        - centred * jnp.mean(scaled * centred, -1, keepdims=True)
    )
    gt_ref[...] = (cot_ref[...].astype(F32) + inner).astype(BF16)
    copy.wait()
    s1[...] = (mine[pl.ds(own, half), :].astype(F32) + rc[...].astype(F32)).astype(BF16)

    quarter = 8 * UNIT
    copies = []
    for d in range(1, 4):
        start = pl.multiple_of(lax.rem(x + d, 4) * quarter, quarter)
        copies.append(send(s1.at[pl.ds(start, quarter)], r1.at[d - 1], d, on_x(d)))
    total = s1[pl.ds(pl.multiple_of(x * quarter, quarter), quarter), :].astype(F32)
    for d in range(1, 4):
        copies[d - 1].wait()
        total += r1[d - 1].astype(F32)
    s2[...] = total.astype(BF16)

    copies = []
    for d in range(1, 8):
        start = pl.multiple_of(lax.rem(p + d, 8) * UNIT, UNIT)
        copies.append(send(s2.at[pl.ds(start, UNIT)], r2.at[d - 1], 3 + d, on_first(d)))
    total = s2[pl.ds(pl.multiple_of(p * UNIT, UNIT), UNIT), :].astype(F32)
    for d in range(1, 8):
        copies[d - 1].wait()
        total += r2[d - 1].astype(F32)
    s3[...] = total.astype(BF16)

    copies = []
    for d in range(1, 8):
        copies.append(send(s3, r3.at[q], 10 + d, on_second(d)))
    r3[q] = s3[...]
    for copy in copies:
        copy.wait()
    total = r3[0].astype(F32)
    for k in range(1, 8):
        total += r3[k].astype(F32)
    block = pl.ds(pl.multiple_of(core * half + x * quarter + p * UNIT, UNIT), UNIT)
    full[block, :] = total.astype(BF16)

    copies = []
    for d in range(1, 8):
        copies.append(send(full.at[block], full.at[block], 17 + d, on_first(d)))
    for copy in copies:
        copy.wait()
    block = pl.ds(pl.multiple_of(core * half + x * quarter, quarter), quarter)
    copies = []
    for d in range(1, 4):
        copies.append(send(full.at[block], full.at[block], 24 + d, on_x(d)))
    last = [send(full.at[block], full.at[block], 28, on_core())]
    for d in range(1, 4):
        copies[d - 1].wait()
        source = lax.rem(x + 4 - d, 4)
        block = pl.ds(pl.multiple_of(core * half + source * quarter, quarter), quarter)
        last.append(send(full.at[block], full.at[block], 28 + d, on_core()))
    for copy in last:
        copy.wait()

    for c in range(3 * width // 128):
        oq_ref[:, c * 128:(c + 1) * 128] = full[c * width:(c + 1) * width, :].astype(F32) * factor
    done = 3 * width // 128 * width
    for c in range(width // 128):
        rows = slice(done + c * width, done + (c + 1) * width)
        oo_ref[:, c * 128:(c + 1) * 128] = full[rows, :].astype(F32) * factor
    done += width // 128 * width
    og_ref[...] = full[done:done + 16, :].astype(F32) * factor


def reduce(factor, tokens, cotangent, gain, weight, grad_q, grad_kv, attended):
    count, width = tokens.shape
    vmem = pl.BlockSpec(memory_space=pltpu.VMEM)
    half = 32 * UNIT

    def body(*refs):
        reduce_kernel(factor, *refs)

    return pl.pallas_call(
        body,
        out_shape=(
            jax.ShapeDtypeStruct((count, width), BF16),
            jax.ShapeDtypeStruct((width, 3 * width), F32),
            jax.ShapeDtypeStruct((width, width), F32),
            jax.ShapeDtypeStruct((16, 128), F32),
        ),
        in_specs=[vmem] * 7,
        out_specs=(vmem,) * 4,
        scratch_shapes=[
            pltpu.VMEM((2 * half, 128), BF16),
            pltpu.VMEM((half, 128), BF16),
            pltpu.VMEM((half, 128), BF16),
            pltpu.VMEM((3, 8 * UNIT, 128), BF16),
            pltpu.VMEM((8 * UNIT, 128), BF16),
            pltpu.VMEM((7, UNIT, 128), BF16),
            pltpu.VMEM((UNIT, 128), BF16),
            pltpu.VMEM((8, UNIT, 128), BF16),
            pltpu.VMEM((2 * half, 128), BF16),
            pltpu.VMEM((16, 128), F32),
            pltpu.SemaphoreType.DMA((32,)),
            pltpu.SemaphoreType.DMA((32,)),
        ],
        compiler_params=pltpu.CompilerParams(
            collective_id=0, has_side_effects=True, vmem_limit_bytes=48 << 20
        ),
        name="weight_grads_all_reduce",
    )(tokens, cotangent, gain, weight, grad_q, grad_kv, attended)


def on_device(tokens, cotangent, key_blocks, qkv_weight, out_weight, norm_gain):
    width = tokens.shape[-1]
    rows = tokens.reshape(-1, width)
    count = rows.shape[0]
    _, centred, _ = norm_parts(rows)
    normed = (centred * norm_gain).astype(BF16)
    projected = jnp.dot(normed, qkv_weight, preferred_element_type=F32).astype(BF16)
    queries = projected[:, :width]
    keyvals = projected[:, width:]
    neighbourhood = extended(
        keyvals.reshape(1, 1, count, 2 * width), (("tm", 0), ("height", 1)), 1
    )
    block_list = key_blocks.reshape(key_blocks.shape[2], key_blocks.shape[3])
    blocks = block_list.shape[0]
    neighbourhood = neighbourhood.reshape(9 * blocks, count // blocks, 2 * width)
    cot_rows = cotangent.reshape(-1, width)
    grad_attended = dot_general(cot_rows, out_weight, 1, 1).astype(BF16)
    attended, grad_queries, key_terms, layer_rows = attention(
        block_list, queries, grad_attended, neighbourhood, rows, out_weight
    )
    pieces = key_terms.reshape(3, 3, count, 2 * width)
    from_below = shifted(pieces[:, 2], "height", 1)
    from_above = shifted(pieces[:, 0], "height", -1)
    sectioned = jnp.stack([pieces[:, 1], from_below, from_above], axis=1)
    from_earlier = shifted(sectioned[2], "tm", 1)
    from_later = shifted(sectioned[0], "tm", -1)
    summed_terms = (
        jnp.sum(sectioned[1].astype(F32), 0)
        + jnp.sum(from_earlier.astype(F32), 0)
        + jnp.sum(from_later.astype(F32), 0)
    )
    grad_keyvals = summed_terms.astype(BF16)
    factor = 1.0 / math.sqrt(count * lax.axis_size("tm") * lax.axis_size("height"))
    grad_tokens, grad_qkv, grad_out, grad_gain = reduce(
        factor, rows, cot_rows, norm_gain.reshape(1, width), qkv_weight,
        grad_queries, grad_keyvals, attended,
    )
    return (
        layer_rows.reshape(tokens.shape),
        grad_tokens.reshape(tokens.shape),
        grad_qkv,
        grad_out,
        grad_gain[:width // 128].reshape(width),
    )


def solution(mesh):
    split = P("tm", "height", None, None)
    return jax.shard_map(
        on_device, mesh=mesh,
        in_specs=(split, split, split, P(), P(), P()),
        out_specs=(split, split, P(), P(), P()),
        check_vma=False,
    )
```

```python
import math

import jax
import jax.numpy as jnp
from jax import lax
from jax.experimental import pallas as pl
from jax.experimental.pallas import tpu as pltpu
from jax.sharding import PartitionSpec as P

HEADS = 6
EPSILON = 1e-05
F32 = jnp.float32
BF16 = jnp.bfloat16
MESH = pl.DeviceIdType.MESH
EARLY = 144
LATE = 160


def norm_parts(token_rows):
    values_in = token_rows.astype(F32)
    center = jnp.mean(values_in, -1, keepdims=True)
    spread = jnp.mean(jnp.square(values_in - center), -1, keepdims=True)
    inverse_scale = lax.rsqrt(spread + EPSILON)
    centred = (values_in - center) * inverse_scale
    return values_in, centred, inverse_scale


def dot_general(a, b, ca, cb):
    return lax.dot_general(a, b, (((ca,), (cb,)), ((), ())), preferred_element_type=F32)


def attention_kernel(list_ref, q_ref, ga_ref, nb_ref, tok_ref, ow_ref,
                     att_ref, gq_ref, terms_ref, lo_ref, acc, kv):
    blocks, length = list_ref.shape
    rows = nb_ref.shape[1]
    width = q_ref.shape[1]
    scale = 1.0 / math.sqrt(width // HEADS)
    acc[...] = jnp.zeros_like(acc)
    first = lax.broadcasted_iota(jnp.int32, (rows, 128), 1) < 64
    zero = jnp.zeros((rows, 128), BF16)

    def split(pair):
        return jnp.concatenate([jnp.where(first, pair, zero), jnp.where(first, zero, pair)], 0)

    def join(both):
        return jnp.where(first, both[:rows], both[rows:])

    def body(n, carry):
        at = pl.multiple_of(n * rows, rows)
        for j in range(length):
            kv[j * rows:(j + 1) * rows, :] = nb_ref[list_ref[n, j]]
        for p in range(width // 128):
            lanes = slice(p * 128, (p + 1) * 128)
            vlanes = slice(width + p * 128, width + (p + 1) * 128)
            qs = split(q_ref[pl.ds(at, rows), lanes])
            gs = split(ga_ref[pl.ds(at, rows), lanes])
            keys = kv[:, lanes]
            values = kv[:, vlanes]
            scores = dot_general(keys, qs, 1, 1) * scale
            top = jnp.max(scores, 0, keepdims=True)
            raw = jnp.exp(scores - top)
            full = raw / jnp.sum(raw, 0, keepdims=True)
            low = full.astype(BF16)
            att_ref[pl.ds(at, rows), lanes] = join(dot_general(low, values, 0, 0)).astype(BF16)
            probs = dot_general(values, gs, 1, 1)
            dots = jnp.sum(full * probs, 0, keepdims=True)
            grad = (full * (probs - dots) * scale).astype(BF16)
            gq_ref[pl.ds(at, rows), lanes] = join(dot_general(grad, keys, 0, 0)).astype(BF16)
            gk = dot_general(grad, qs, 1, 0)
            gv = dot_general(low, gs, 1, 0)
            for j in range(length):
                b = list_ref[n, j]
                part = slice(j * rows, (j + 1) * rows)
                acc[b, :, lanes] = acc[b, :, lanes] + gk[part]
                acc[b, :, vlanes] = acc[b, :, vlanes] + gv[part]
        return carry

    lax.fori_loop(0, blocks, body, 0)
    terms_ref[...] = acc[...].astype(BF16)
    out = dot_general(att_ref[...], ow_ref[...], 1, 0)
    lo_ref[...] = (tok_ref[...].astype(F32) + out).astype(BF16)


def attention(block_list, queries, grad_attended, neighbourhood, tokens, out_weight):
    count, width = queries.shape
    blocks = block_list.shape[0]
    rows = count // blocks
    vmem = pl.BlockSpec(memory_space=pltpu.VMEM)
    return pl.pallas_call(
        attention_kernel,
        out_shape=(
            jax.ShapeDtypeStruct((count, width), BF16),
            jax.ShapeDtypeStruct((count, width), BF16),
            jax.ShapeDtypeStruct((9 * blocks, rows, 2 * width), BF16),
            jax.ShapeDtypeStruct((count, width), BF16),
        ),
        in_specs=[pl.BlockSpec(memory_space=pltpu.SMEM)] + [vmem] * 5,
        out_specs=(vmem,) * 4,
        scratch_shapes=[
            pltpu.VMEM((9 * blocks, rows, 2 * width), F32),
            pltpu.VMEM((block_list.shape[1] * rows, 2 * width), BF16),
        ],
        compiler_params=pltpu.CompilerParams(vmem_limit_bytes=48 << 20),
        name="sparse_attention",
    )(block_list, queries, grad_attended, neighbourhood, tokens, out_weight)


def place():
    t = lax.axis_index("tm")
    h = lax.axis_index("height")
    return t // 8, lax.rem(t, 8), h // 4, lax.rem(h // 2, 2), lax.rem(h, 2)


def device(x, y, z, core):
    return ((x // 2) * 8 + y, z * 4 + lax.rem(x, 2) * 2 + core)


class Grid:
    def __init__(self):
        self.t = lax.axis_index("tm")
        self.h = lax.axis_index("height")
        self.core = lax.rem(self.h, 2)
        step = 2 * self.core - 1
        self.partner = (self.t, self.h - step)
        self.outer = (self.t, self.h + step)
        self.before = (self.t - 1, self.h)
        self.after = (self.t + 1, self.h)
        top = lax.axis_size("height") - 1
        self.has_outer = jnp.logical_and(self.h + step >= 0, self.h + step <= top)
        self.has_before = self.t > 0
        self.has_after = self.t < lax.axis_size("tm") - 1

    def greet(self, barrier):
        for there, target in ((self.has_outer, self.outer), (self.has_before, self.before),
                              (self.has_after, self.after)):
            @pl.when(there)
            def _():
                pl.semaphore_signal(barrier, inc=1, device_id=target, device_id_type=MESH)

    def meet(self, barrier, peers):
        number = jnp.int32(peers)
        for there in (self.has_outer, self.has_before, self.has_after):
            number += there.astype(jnp.int32)
        pl.semaphore_wait(barrier, number)


def remote(src, dst, ssem, rsem, slot, target):
    return pltpu.make_async_remote_copy(
        src_ref=src, dst_ref=dst, send_sem=ssem.at[slot], recv_sem=rsem.at[slot],
        device_id=target, device_id_type=MESH,
    )


def both(a, b):
    return jnp.logical_and(a, b)


def project_kernel(tok_ref, cot_ref, gain_ref, w_ref, ow_ref, q_ref, ga_ref, nb, ssem, rsem):
    width = tok_ref.shape[1]
    g = Grid()
    core = g.core
    barrier = pltpu.get_barrier_semaphore()
    pl.semaphore_signal(barrier, inc=1, device_id=g.partner, device_id_type=MESH)
    g.greet(barrier)
    _, centred, _ = norm_parts(tok_ref[...])
    normed = (centred * gain_ref[...]).astype(BF16)
    nb[4] = dot_general(normed, w_ref[:, width:], 1, 0).astype(BF16)
    g.meet(barrier, 1)

    far = 3 + 2 * core
    near = 3 + 2 * (1 - core)

    def copy(src, dst, slot, target):
        return remote(nb.at[src], nb.at[dst], ssem, rsem, slot, target)

    to_outer = copy(4, near, 1, g.outer)
    up = copy(4, 1, 2, g.after)
    down = copy(4, 7, 3, g.before)
    to_partner = copy(4, far, 0, g.partner)
    up_outer = copy(far, 2 * core, 4, g.after)
    down_outer = copy(far, 6 + 2 * core, 5, g.before)
    low_partner = copy(1, 2 * core, 6, g.partner)
    high_partner = copy(7, 6 + 2 * core, 7, g.partner)

    pl.when(g.has_outer)(to_outer.start)
    pl.when(g.has_after)(up.start)
    pl.when(g.has_before)(down.start)
    to_partner.start()
    q_ref[...] = dot_general(normed, w_ref[:, :width], 1, 0).astype(BF16)
    ga_ref[...] = dot_general(cot_ref[...], ow_ref[...], 1, 1).astype(BF16)
    to_partner.wait()
    pl.when(g.has_outer)(to_outer.wait)
    pl.when(both(g.has_outer, g.has_after))(up_outer.start)
    pl.when(both(g.has_outer, g.has_before))(down_outer.start)

    @pl.when(g.has_before)
    def _():
        up.wait_recv()
        low_partner.start()

    @pl.when(g.has_after)
    def _():
        down.wait_recv()
        high_partner.start()

    pl.when(g.has_after)(up.wait_send)
    pl.when(g.has_before)(down.wait_send)
    pl.when(both(g.has_outer, g.has_after))(up_outer.wait_send)
    pl.when(both(g.has_outer, g.has_before))(up_outer.wait_recv)
    pl.when(both(g.has_outer, g.has_before))(down_outer.wait_send)
    pl.when(both(g.has_outer, g.has_after))(down_outer.wait_recv)
    pl.when(g.has_before)(low_partner.wait)
    pl.when(g.has_after)(high_partner.wait)


def project(tokens, cotangent, gain, weight, out_weight):
    count, width = tokens.shape
    vmem = pl.BlockSpec(memory_space=pltpu.VMEM)
    return pl.pallas_call(
        project_kernel,
        out_shape=(
            jax.ShapeDtypeStruct((count, width), BF16),
            jax.ShapeDtypeStruct((count, width), BF16),
            jax.ShapeDtypeStruct((9, count, 2 * width), BF16),
        ),
        in_specs=[vmem] * 5,
        out_specs=(vmem,) * 3,
        scratch_shapes=[pltpu.SemaphoreType.DMA((8,)), pltpu.SemaphoreType.DMA((8,))],
        compiler_params=pltpu.CompilerParams(
            collective_id=1, has_side_effects=True, vmem_limit_bytes=40 << 20
        ),
        name="project_and_halo",
    )(tokens, cotangent, gain, weight, out_weight)


class Peers:
    def __init__(self):
        x_hi, self.y, self.z, x_lo, self.core = place()
        self.x = x_hi * 2 + x_lo
        self.p = jnp.where(self.core == 0, self.z, self.y)
        self.q = jnp.where(self.core == 0, self.y, self.z)

    def on_core(self):
        return device(self.x, self.y, self.z, 1 - self.core)

    def on_x(self, d):
        return device(lax.rem(self.x + d, 4), self.y, self.z, self.core)

    def on_first(self, d):
        there = lax.rem(self.p + d, 8)
        return device(self.x, jnp.where(self.core == 0, self.y, there),
                      jnp.where(self.core == 0, there, self.z), self.core)

    def on_second(self, d):
        there = lax.rem(self.q + d, 8)
        return device(self.x, jnp.where(self.core == 0, there, self.y),
                      jnp.where(self.core == 0, self.z, there), self.core)


class Reduction:
    def __init__(self, peers, unit, mine, rc, s1, r1, s2, r2, s3, r3, full, ssem, rsem):
        self.peers, self.unit, self.half = peers, unit, 8 * unit
        self.mine, self.rc, self.s1, self.r1, self.s2, self.r2 = mine, rc, s1, r1, s2, r2
        self.s3, self.r3, self.full, self.ssem, self.rsem = s3, r3, full, ssem, rsem

    @staticmethod
    def scratch(unit):
        half = 8 * unit
        return [
            pltpu.VMEM((2 * half, 128), BF16),
            pltpu.VMEM((half, 128), BF16),
            pltpu.VMEM((half, 128), BF16),
            pltpu.VMEM((7, unit, 128), BF16),
            pltpu.VMEM((unit, 128), BF16),
            pltpu.VMEM((8, unit, 128), BF16),
            pltpu.VMEM((unit, 128), BF16),
            pltpu.VMEM((4, unit, 128), BF16),
            pltpu.VMEM((2 * half, 128), BF16),
            pltpu.SemaphoreType.DMA((33,)),
            pltpu.SemaphoreType.DMA((33,)),
        ]

    def send(self, src, dst, slot, target):
        copy = remote(src, dst, self.ssem, self.rsem, slot, target)
        copy.start()
        return copy

    def rows(self, core, p):
        return pl.ds(pl.multiple_of(core * self.half + p * self.unit, 16), self.unit)

    def half_rows(self, core):
        return pl.ds(pl.multiple_of(core * self.half, 16), self.half)

    def start_core(self):
        k = self.peers
        self.copy = self.send(self.mine.at[self.half_rows(1 - k.core)], self.rc, 0, k.on_core())

    def start_scatter(self):
        k = self.peers
        self.copy.wait()
        own = self.mine[self.half_rows(k.core), :].astype(F32)
        self.s1[...] = (own + self.rc[...].astype(F32)).astype(BF16)
        self.copies = [
            self.send(self.s1.at[self.rows(0, lax.rem(k.p + d, 8))], self.r1.at[d - 1], d, k.on_first(d))
            for d in range(1, 8)
        ]

    def start_second(self):
        k = self.peers
        total = self.s1[self.rows(0, k.p), :].astype(F32)
        for d in range(1, 8):
            self.copies[d - 1].wait()
            total += self.r1[d - 1].astype(F32)
        self.s2[...] = total.astype(BF16)
        self.copies = [
            self.send(self.s2, self.r2.at[k.q], 7 + d, k.on_second(d)) for d in range(1, 8)
        ]
        self.r2[k.q] = self.s2[...]

    def start_x(self):
        k = self.peers
        for copy in self.copies:
            copy.wait()
        total = self.r2[0].astype(F32)
        for i in range(1, 8):
            total += self.r2[i].astype(F32)
        self.s3[...] = total.astype(BF16)
        self.copies = [self.send(self.s3, self.r3.at[k.x], 14 + d, k.on_x(d)) for d in range(1, 4)]
        self.r3[k.x] = self.s3[...]

    def start_gather(self):
        k = self.peers
        for copy in self.copies:
            copy.wait()
        total = self.r3[0].astype(F32)
        for i in range(1, 4):
            total += self.r3[i].astype(F32)
        block = self.rows(k.core, k.p)
        self.full[block, :] = total.astype(BF16)
        piece = self.full.at[block]
        self.copies = [self.send(piece, piece, 17 + d, k.on_first(d)) for d in range(1, 8)]
        self.last = [self.send(piece, piece, 25, k.on_core())]

    def forward(self):
        k = self.peers
        for d in range(1, 8):
            self.copies[d - 1].wait()
            piece = self.full.at[self.rows(k.core, lax.rem(k.p + 8 - d, 8))]
            self.last.append(self.send(piece, piece, 25 + d, k.on_core()))

    def finish(self):
        for copy in self.last:
            copy.wait()


def reduce_kernel(factor, tok_ref, cot_ref, gain_ref, w_ref, gq_ref, terms, att_ref,
                  gt_ref, oq_ref, oo_ref, og_ref,
                  part, ysum, youter, sums, osum, xin, acc, gkv, grad_normed, small,
                  tsem, usem, *rest):
    width = tok_ref.shape[1]
    n = width // 128
    g = Grid()
    core = g.core
    k = Peers()
    early = Reduction(k, EARLY, *rest[:11])
    late = Reduction(k, LATE, *rest[11:])

    barrier = pltpu.get_barrier_semaphore()
    targets = [k.on_core()] + [k.on_x(d) for d in range(1, 4)]
    targets += [k.on_first(d) for d in range(1, 8)] + [k.on_second(d) for d in range(1, 8)]
    for target in targets:
        pl.semaphore_signal(barrier, inc=1, device_id=target, device_id_type=MESH)
    g.greet(barrier)
    g.meet(barrier, len(targets))

    def copy(src, dst, slot, target):
        return remote(src, dst, tsem, usem, slot, target)

    outer_down = copy(terms.at[2 * core], youter.at[0], 0, g.before)
    outer_up = copy(terms.at[6 + 2 * core], youter.at[1], 1, g.after)
    pl.when(both(g.has_outer, g.has_before))(outer_down.start)
    pl.when(both(g.has_outer, g.has_after))(outer_up.start)
    to_partner = {}
    for a in (0, 2, 1):
        to_partner[a] = copy(terms.at[3 * a + 2 * (1 - core)], part.at[a], 2 + a, g.partner)
        to_partner[a].start()

    _, centred, inverse = norm_parts(tok_ref[...])
    gain = gain_ref[...]
    normed_t = (centred * gain).astype(BF16).T
    att_t = att_ref[...].T
    for c in range(n):
        lanes = slice(c * 128, (c + 1) * 128)
        early.mine[c * width:(c + 1) * width, :] = dot_general(normed_t, gq_ref[:, lanes], 1, 0).astype(BF16)
        early.mine[(n + c) * width:(n + c + 1) * width, :] = dot_general(
            att_t, cot_ref[:, lanes], 1, 0).astype(BF16)

    to_partner[0].wait()
    sums[0] = (terms[1].astype(F32) + part[0].astype(F32)).astype(BF16)
    down = copy(sums.at[0], ysum.at[0], 5, g.before)
    pl.when(g.has_before)(down.start)
    to_partner[2].wait()
    sums[1] = (terms[7].astype(F32) + part[2].astype(F32)).astype(BF16)
    up = copy(sums.at[1], ysum.at[1], 6, g.after)
    pl.when(g.has_after)(up.start)
    early.start_core()
    grad_normed[...] = dot_general(gq_ref[...], w_ref[:, :width], 1, 1)
    to_partner[1].wait()
    early.start_scatter()

    outward = copy(osum, xin, 7, g.outer)

    @pl.when(g.has_outer)
    def _():
        acc[...] = terms[3 + 2 * core].astype(F32)

        @pl.when(g.has_after)
        def _():
            outer_down.wait_recv()
            acc[...] += youter[0].astype(F32)

        @pl.when(g.has_before)
        def _():
            outer_up.wait_recv()
            acc[...] += youter[1].astype(F32)

        osum[...] = acc[...].astype(BF16)
        outward.start()

    early.start_second()
    acc[...] = terms[4].astype(F32) + part[1].astype(F32)

    @pl.when(g.has_after)
    def _():
        down.wait_recv()
        acc[...] += ysum[0].astype(F32)

    @pl.when(g.has_before)
    def _():
        up.wait_recv()
        acc[...] += ysum[1].astype(F32)

    early.start_x()

    @pl.when(g.has_outer)
    def _():
        outward.wait()
        acc[...] += xin[...].astype(F32)

    gkv[...] = acc[...].astype(BF16)
    for c in range(2 * n):
        late.mine[c * width:(c + 1) * width, :] = dot_general(
            normed_t, gkv[:, c * 128:(c + 1) * 128], 1, 0).astype(BF16)
    total = grad_normed[...] + dot_general(gkv[...], w_ref[:, width:], 1, 1)
    local_gain = jnp.sum(total * centred, 0, keepdims=True)
    small[...] = jnp.zeros_like(small)
    for c in range(n):
        small[c:c + 1, :] = local_gain[:, c * 128:(c + 1) * 128]
    at = 2 * n * width
    late.mine[at:at + 16, :] = small[...].astype(BF16)
    late.mine[at + 16:, :] = jnp.zeros((16 * LATE - at - 16, 128), BF16)
    late.start_core()
    early.start_gather()
    scaled = total * gain
    inner = inverse * (
        scaled
        - jnp.mean(scaled, -1, keepdims=True)
        - centred * jnp.mean(scaled * centred, -1, keepdims=True)
    )
    gt_ref[...] = (cot_ref[...].astype(F32) + inner).astype(BF16)
    late.start_scatter()
    early.forward()
    late.start_second()
    early.finish()
    for c in range(n):
        lanes = slice(c * 128, (c + 1) * 128)
        oq_ref[:, lanes] = early.full[c * width:(c + 1) * width, :].astype(F32) * factor
        oo_ref[:, lanes] = early.full[(n + c) * width:(n + c + 1) * width, :].astype(F32) * factor
    late.start_x()
    late.start_gather()
    late.forward()
    late.finish()
    for c in range(2 * n):
        lanes = slice((n + c) * 128, (n + c + 1) * 128)
        oq_ref[:, lanes] = late.full[c * width:(c + 1) * width, :].astype(F32) * factor
    og_ref[...] = late.full[at:at + 16, :].astype(F32) * factor
    pl.when(both(g.has_outer, g.has_before))(outer_down.wait_send)
    pl.when(both(g.has_outer, g.has_after))(outer_up.wait_send)
    pl.when(g.has_before)(down.wait_send)
    pl.when(g.has_after)(up.wait_send)


def reduce(factor, tokens, cotangent, gain, weight, grad_q, terms, attended):
    count, width = tokens.shape
    vmem = pl.BlockSpec(memory_space=pltpu.VMEM)
    tile = (count, 2 * width)

    def body(*refs):
        reduce_kernel(factor, *refs)

    return pl.pallas_call(
        body,
        out_shape=(
            jax.ShapeDtypeStruct((count, width), BF16),
            jax.ShapeDtypeStruct((width, 3 * width), F32),
            jax.ShapeDtypeStruct((width, width), F32),
            jax.ShapeDtypeStruct((16, 128), F32),
        ),
        in_specs=[vmem] * 7,
        out_specs=(vmem,) * 4,
        scratch_shapes=[
            pltpu.VMEM((3,) + tile, BF16),
            pltpu.VMEM((2,) + tile, BF16),
            pltpu.VMEM((2,) + tile, BF16),
            pltpu.VMEM((2,) + tile, BF16),
            pltpu.VMEM(tile, BF16),
            pltpu.VMEM(tile, BF16),
            pltpu.VMEM(tile, F32),
            pltpu.VMEM(tile, BF16),
            pltpu.VMEM((count, width), F32),
            pltpu.VMEM((16, 128), F32),
            pltpu.SemaphoreType.DMA((8,)),
            pltpu.SemaphoreType.DMA((8,)),
        ] + Reduction.scratch(EARLY) + Reduction.scratch(LATE),
        compiler_params=pltpu.CompilerParams(
            collective_id=0, has_side_effects=True, vmem_limit_bytes=48 << 20
        ),
        name="key_terms_and_all_reduce",
    )(tokens, cotangent, gain, weight, grad_q, terms, attended)


def on_device(tokens, cotangent, key_blocks, qkv_weight, out_weight, norm_gain):
    width = tokens.shape[-1]
    rows = tokens.reshape(-1, width)
    count = rows.shape[0]
    gain = norm_gain.reshape(1, width)
    cot_rows = cotangent.reshape(-1, width)
    block_list = key_blocks.reshape(key_blocks.shape[2], key_blocks.shape[3])
    blocks = block_list.shape[0]
    queries, grad_attended, neighbourhood = project(rows, cot_rows, gain, qkv_weight, out_weight)
    attended, grad_queries, key_terms, layer_rows = attention(
        block_list, queries, grad_attended,
        neighbourhood.reshape(9 * blocks, count // blocks, 2 * width), rows, out_weight,
    )
    factor = 1.0 / math.sqrt(count * lax.axis_size("tm") * lax.axis_size("height"))
    grad_tokens, grad_qkv, grad_out, grad_gain = reduce(
        factor, rows, cot_rows, gain, qkv_weight, grad_queries,
        key_terms.reshape(9, count, 2 * width), attended,
    )
    return (
        layer_rows.reshape(tokens.shape),
        grad_tokens.reshape(tokens.shape),
        grad_qkv,
        grad_out,
        grad_gain[:width // 128].reshape(width),
    )


def solution(mesh):
    split = P("tm", "height", None, None)
    return jax.shard_map(
        on_device, mesh=mesh,
        in_specs=(split, split, split, P(), P(), P()),
        out_specs=(split, split, P(), P(), P()),
        check_vma=False,
    )
```

```python
import math

import jax
import jax.numpy as jnp
from jax import lax
from jax.experimental import pallas as pl
from jax.experimental.pallas import tpu as pltpu
from jax.sharding import PartitionSpec as P

HEADS = 6
EPSILON = 1e-05
F32 = jnp.float32
BF16 = jnp.bfloat16
MESH = pl.DeviceIdType.MESH
UNIT = 144
LIMIT = 28 << 20
VMEM = pl.BlockSpec(memory_space=pltpu.VMEM)
HBM = pl.BlockSpec(memory_space=pltpu.HBM)


def norm_parts(token_rows):
    values_in = token_rows.astype(F32)
    center = jnp.mean(values_in, -1, keepdims=True)
    spread = jnp.mean(jnp.square(values_in - center), -1, keepdims=True)
    inverse_scale = lax.rsqrt(spread + EPSILON)
    centred = (values_in - center) * inverse_scale
    return values_in, centred, inverse_scale


def dot_general(a, b, ca, cb):
    return lax.dot_general(a, b, (((ca,), (cb,)), ((), ())), preferred_element_type=F32)


def attention_kernel(list_ref, q_ref, ga_ref, nb_ref, normed_ref, tok_hbm, cot_hbm, ow_hbm,
                     gq_ref, terms_ref, lo_ref, mine_ref,
                     acc, kv, att_ref, grads, tok_ref, cot_ref, ow_ref, sem):
    loads = [
        pltpu.make_async_copy(src, dst, sem.at[i])
        for i, (src, dst) in enumerate(((tok_hbm, tok_ref), (cot_hbm, cot_ref), (ow_hbm, ow_ref)))
    ]
    for load in loads:
        load.start()
    blocks, length = list_ref.shape
    rows = nb_ref.shape[1]
    width = q_ref.shape[1]
    scale = 1.0 / math.sqrt(width // HEADS)
    acc[...] = jnp.zeros_like(acc)
    first = lax.broadcasted_iota(jnp.int32, (rows, 128), 1) < 64
    zero = jnp.zeros((rows, 128), BF16)

    def split(pair):
        return jnp.concatenate([jnp.where(first, pair, zero), jnp.where(first, zero, pair)], 0)

    def join(both):
        return jnp.where(first, both[:rows], both[rows:])

    def body(n, carry):
        at = pl.multiple_of(n * rows, rows)
        for j in range(length):
            kv[j * rows:(j + 1) * rows, :] = nb_ref[list_ref[n, j]]
        for p in range(width // 128):
            lanes = slice(p * 128, (p + 1) * 128)
            vlanes = slice(width + p * 128, width + (p + 1) * 128)
            qs = split(q_ref[pl.ds(at, rows), lanes])
            gs = split(ga_ref[pl.ds(at, rows), lanes])
            keys = kv[:, lanes]
            values = kv[:, vlanes]
            scores = dot_general(keys, qs, 1, 1) * scale
            top = jnp.max(scores, 0, keepdims=True)
            raw = jnp.exp(scores - top)
            full = raw / jnp.sum(raw, 0, keepdims=True)
            low = full.astype(BF16)
            att_ref[pl.ds(at, rows), lanes] = join(dot_general(low, values, 0, 0)).astype(BF16)
            probs = dot_general(values, gs, 1, 1)
            dots = jnp.sum(full * probs, 0, keepdims=True)
            grad = (full * (probs - dots) * scale).astype(BF16)
            gq_ref[pl.ds(at, rows), lanes] = join(dot_general(grad, keys, 0, 0)).astype(BF16)
            gk = dot_general(grad, qs, 1, 0)
            gv = dot_general(low, gs, 1, 0)
            for j in range(length):
                b = list_ref[n, j]
                part = slice(j * rows, (j + 1) * rows)
                acc[b, :, lanes] = acc[b, :, lanes] + gk[part]
                acc[b, :, vlanes] = acc[b, :, vlanes] + gv[part]
        return carry

    lax.fori_loop(0, blocks, body, 0)
    terms_ref[...] = acc[...].astype(BF16)
    n = width // 128
    tile = blocks * rows
    grads[...] = jnp.zeros_like(grads)

    def add_tile(i, carry):
        normed_t = normed_ref[i].T
        keys = terms_ref[pl.ds(i * blocks, blocks)].reshape(tile, 2 * width)
        grads[...] += dot_general(normed_t, keys, 1, 0)
        return carry

    lax.fori_loop(0, 9, add_tile, 0)
    normed_t = normed_ref[4].T
    for load in loads:
        load.wait()
    att_t = att_ref[...].T
    for c in range(n):
        lanes = slice(c * 128, (c + 1) * 128)
        mine_ref[c * width:(c + 1) * width, :] = dot_general(
            normed_t, gq_ref[:, lanes], 1, 0).astype(BF16)
        mine_ref[(3 * n + c) * width:(3 * n + c + 1) * width, :] = dot_general(
            att_t, cot_ref[:, lanes], 1, 0).astype(BF16)
    for c in range(2 * n):
        mine_ref[(n + c) * width:(n + c + 1) * width, :] = grads[:, c * 128:(c + 1) * 128].astype(BF16)
    out = dot_general(att_ref[...], ow_ref[...], 1, 0)
    lo_ref[...] = (tok_ref[...].astype(F32) + out).astype(BF16)


def attention(block_list, queries, grad_attended, neighbourhood, normed, tokens, cotangent, out_weight):
    count, width = queries.shape
    blocks = block_list.shape[0]
    rows = count // blocks
    return pl.pallas_call(
        attention_kernel,
        out_shape=(
            jax.ShapeDtypeStruct((count, width), BF16),
            jax.ShapeDtypeStruct((9 * blocks, rows, 2 * width), BF16),
            jax.ShapeDtypeStruct((count, width), BF16),
            jax.ShapeDtypeStruct((4 * width // 128 * width, 128), BF16),
        ),
        in_specs=[pl.BlockSpec(memory_space=pltpu.SMEM)] + [VMEM] * 4 + [HBM] * 3,
        out_specs=(VMEM,) * 4,
        scratch_shapes=[
            pltpu.VMEM((9 * blocks, rows, 2 * width), F32),
            pltpu.VMEM((block_list.shape[1] * rows, 2 * width), BF16),
            pltpu.VMEM((count, width), BF16),
            pltpu.VMEM((width, 2 * width), F32),
            pltpu.VMEM((count, width), BF16),
            pltpu.VMEM((count, width), BF16),
            pltpu.VMEM((width, width), BF16),
            pltpu.SemaphoreType.DMA((3,)),
        ],
        compiler_params=pltpu.CompilerParams(vmem_limit_bytes=LIMIT),
        name="sparse_attention",
    )(block_list, queries, grad_attended, neighbourhood, normed, tokens, cotangent, out_weight)


def place():
    t = lax.axis_index("tm")
    h = lax.axis_index("height")
    return t // 8, lax.rem(t, 8), h // 4, lax.rem(h // 2, 2), lax.rem(h, 2)


def device(x, y, z, core):
    return ((x // 2) * 8 + y, z * 4 + lax.rem(x, 2) * 2 + core)


class Grid:
    def __init__(self):
        self.t = lax.axis_index("tm")
        self.h = lax.axis_index("height")
        self.core = lax.rem(self.h, 2)
        step = 2 * self.core - 1
        self.partner = (self.t, self.h - step)
        self.outer = (self.t, self.h + step)
        self.before = (self.t - 1, self.h)
        self.after = (self.t + 1, self.h)
        top = lax.axis_size("height") - 1
        self.has_outer = jnp.logical_and(self.h + step >= 0, self.h + step <= top)
        self.has_before = self.t > 0
        self.has_after = self.t < lax.axis_size("tm") - 1

    def greet(self, barrier):
        for there, target in ((self.has_outer, self.outer), (self.has_before, self.before),
                              (self.has_after, self.after)):
            @pl.when(there)
            def _():
                pl.semaphore_signal(barrier, inc=1, device_id=target, device_id_type=MESH)

    def meet(self, barrier, peers):
        number = jnp.int32(peers)
        for there in (self.has_outer, self.has_before, self.has_after):
            number += there.astype(jnp.int32)
        pl.semaphore_wait(barrier, number)


def remote(src, dst, ssem, rsem, slot, target):
    return pltpu.make_async_remote_copy(
        src_ref=src, dst_ref=dst, send_sem=ssem.at[slot], recv_sem=rsem.at[slot],
        device_id=target, device_id_type=MESH,
    )


def both(a, b):
    return jnp.logical_and(a, b)


def project_kernel(tok_hbm, cot_hbm, gain_ref, w_hbm, ow_hbm, q_ref, ga_ref, nb, normed_ref,
                   tiles, cot_ref, w_ref, ow_ref, lsem, ssem, rsem):
    width = q_ref.shape[1]
    g = Grid()
    core = g.core
    barrier = pltpu.get_barrier_semaphore()
    pl.semaphore_signal(barrier, inc=1, device_id=g.partner, device_id_type=MESH)
    g.greet(barrier)
    loads = [
        pltpu.make_async_copy(src, dst, lsem.at[i])
        for i, (src, dst) in enumerate(
            ((tok_hbm, tiles.at[4]), (w_hbm, w_ref), (cot_hbm, cot_ref), (ow_hbm, ow_ref)))
    ]
    for load in loads:
        load.start()
    g.meet(barrier, 1)

    far = 3 + 2 * core
    near = 3 + 2 * (1 - core)

    def copy(src, dst, slot, target):
        return remote(src, tiles.at[dst], ssem, rsem, slot, target)

    to_outer = copy(tok_hbm, near, 1, g.outer)
    up = copy(tok_hbm, 1, 2, g.after)
    down = copy(tok_hbm, 7, 3, g.before)
    to_partner = copy(tok_hbm, far, 0, g.partner)
    up_outer = copy(tiles.at[far], 2 * core, 4, g.after)
    down_outer = copy(tiles.at[far], 6 + 2 * core, 5, g.before)
    low_partner = copy(tiles.at[1], 2 * core, 6, g.partner)
    high_partner = copy(tiles.at[7], 6 + 2 * core, 7, g.partner)
    outer_before = both(g.has_outer, g.has_before)
    outer_after = both(g.has_outer, g.has_after)

    pl.when(g.has_outer)(to_outer.start)
    pl.when(g.has_after)(up.start)
    pl.when(g.has_before)(down.start)
    to_partner.start()

    def fill(slot):
        _, centred, _ = norm_parts(tiles[slot])
        normed = (centred * gain_ref[...]).astype(BF16)
        normed_ref[slot] = normed
        nb[slot] = dot_general(normed, w_ref[:, width:], 1, 0).astype(BF16)
        return normed

    def fill_if(there, slot):
        @pl.when(there)
        def _():
            fill(slot)

        @pl.when(jnp.logical_not(there))
        def _():
            normed_ref[slot] = jnp.zeros_like(normed_ref[slot])

    for load in loads:
        load.wait()
    normed = fill(4)
    q_ref[...] = dot_general(normed, w_ref[:, :width], 1, 0).astype(BF16)
    ga_ref[...] = dot_general(cot_ref[...], ow_ref[...], 1, 1).astype(BF16)
    pl.when(g.has_outer)(to_outer.wait)
    pl.when(outer_after)(up_outer.start)
    pl.when(outer_before)(down_outer.start)

    @pl.when(g.has_before)
    def _():
        up.wait_recv()
        low_partner.start()

    @pl.when(g.has_after)
    def _():
        down.wait_recv()
        high_partner.start()

    to_partner.wait()
    fill(near)
    fill_if(g.has_outer, far)
    fill_if(g.has_before, 1)
    fill_if(g.has_after, 7)
    pl.when(g.has_before)(low_partner.wait)
    fill_if(g.has_before, 2 * (1 - core))
    pl.when(g.has_after)(high_partner.wait)
    fill_if(g.has_after, 6 + 2 * (1 - core))
    pl.when(outer_before)(up_outer.wait_recv)
    fill_if(outer_before, 2 * core)
    pl.when(outer_after)(down_outer.wait_recv)
    fill_if(outer_after, 6 + 2 * core)
    pl.when(g.has_after)(up.wait_send)
    pl.when(g.has_before)(down.wait_send)
    pl.when(outer_after)(up_outer.wait_send)
    pl.when(outer_before)(down_outer.wait_send)


def project(tokens, cotangent, gain, weight, out_weight):
    count, width = tokens.shape
    return pl.pallas_call(
        project_kernel,
        out_shape=(
            jax.ShapeDtypeStruct((count, width), BF16),
            jax.ShapeDtypeStruct((count, width), BF16),
            jax.ShapeDtypeStruct((9, count, 2 * width), BF16),
            jax.ShapeDtypeStruct((9, count, width), BF16),
        ),
        in_specs=[HBM, HBM, VMEM, HBM, HBM],
        out_specs=(VMEM,) * 4,
        scratch_shapes=[
            pltpu.VMEM((9, count, width), BF16),
            pltpu.VMEM((count, width), BF16),
            pltpu.VMEM((width, 3 * width), BF16),
            pltpu.VMEM((width, width), BF16),
            pltpu.SemaphoreType.DMA((4,)),
            pltpu.SemaphoreType.DMA((8,)),
            pltpu.SemaphoreType.DMA((8,)),
        ],
        compiler_params=pltpu.CompilerParams(
            collective_id=1, has_side_effects=True, vmem_limit_bytes=LIMIT
        ),
        name="halo_and_project",
    )(tokens, cotangent, gain, weight, out_weight)


class Peers:
    def __init__(self, swap):
        x_hi, self.y, self.z, x_lo, self.core = place()
        self.x = x_hi * 2 + x_lo
        self.along_z = self.core == swap
        self.p = jnp.where(self.along_z, self.z, self.y)
        self.q = jnp.where(self.along_z, self.y, self.z)

    def on_core(self):
        return device(self.x, self.y, self.z, 1 - self.core)

    def on_x(self, d):
        return device(lax.rem(self.x + d, 4), self.y, self.z, self.core)

    def on_first(self, d):
        there = lax.rem(self.p + d, 8)
        return device(self.x, jnp.where(self.along_z, self.y, there),
                      jnp.where(self.along_z, there, self.z), self.core)

    def on_second(self, d):
        there = lax.rem(self.q + d, 8)
        return device(self.x, jnp.where(self.along_z, there, self.y),
                      jnp.where(self.along_z, self.z, there), self.core)


class Reduction:
    def __init__(self, peers, unit, mine, rc, s1, r1, s2, r2, s3, r3, full, ssem, rsem):
        self.peers, self.unit, self.half = peers, unit, 8 * unit
        self.mine, self.rc, self.s1, self.r1, self.s2, self.r2 = mine, rc, s1, r1, s2, r2
        self.s3, self.r3, self.full, self.ssem, self.rsem = s3, r3, full, ssem, rsem

    @staticmethod
    def scratch(unit):
        half = 8 * unit
        return [
            pltpu.VMEM((half, 128), BF16),
            pltpu.VMEM((half, 128), BF16),
            pltpu.VMEM((7, unit, 128), BF16),
            pltpu.VMEM((unit, 128), BF16),
            pltpu.VMEM((8, unit, 128), BF16),
            pltpu.VMEM((unit, 128), BF16),
            pltpu.VMEM((4, unit, 128), BF16),
            pltpu.VMEM((2 * half, 128), BF16),
            pltpu.SemaphoreType.DMA((33,)),
            pltpu.SemaphoreType.DMA((33,)),
        ]

    def send(self, src, dst, slot, target):
        copy = remote(src, dst, self.ssem, self.rsem, slot, target)
        copy.start()
        return copy

    def rows(self, core, p):
        return pl.ds(pl.multiple_of(core * self.half + p * self.unit, 16), self.unit)

    def half_rows(self, core):
        return pl.ds(pl.multiple_of(core * self.half, 16), self.half)

    def start_core(self):
        k = self.peers
        self.copy = self.send(self.mine.at[self.half_rows(1 - k.core)], self.rc, 0, k.on_core())

    def start_scatter(self):
        k = self.peers
        self.copy.wait()
        own = self.mine[self.half_rows(k.core), :].astype(F32)
        self.s1[...] = (own + self.rc[...].astype(F32)).astype(BF16)
        self.copies = [
            self.send(self.s1.at[self.rows(0, lax.rem(k.p + d, 8))], self.r1.at[d - 1], d, k.on_first(d))
            for d in range(1, 8)
        ]

    def start_second(self):
        k = self.peers
        total = self.s1[self.rows(0, k.p), :].astype(F32)
        for d in range(1, 8):
            self.copies[d - 1].wait()
            total += self.r1[d - 1].astype(F32)
        self.s2[...] = total.astype(BF16)
        self.copies = [
            self.send(self.s2, self.r2.at[k.q], 7 + d, k.on_second(d)) for d in range(1, 8)
        ]
        self.r2[k.q] = self.s2[...]

    def start_x(self):
        k = self.peers
        for copy in self.copies:
            copy.wait()
        total = self.r2[0].astype(F32)
        for i in range(1, 8):
            total += self.r2[i].astype(F32)
        self.s3[...] = total.astype(BF16)
        self.copies = [self.send(self.s3, self.r3.at[k.x], 14 + d, k.on_x(d)) for d in range(1, 4)]
        self.r3[k.x] = self.s3[...]

    def start_gather(self):
        k = self.peers
        for copy in self.copies:
            copy.wait()
        total = self.r3[0].astype(F32)
        for i in range(1, 4):
            total += self.r3[i].astype(F32)
        block = self.rows(k.core, k.p)
        self.full[block, :] = total.astype(BF16)
        piece = self.full.at[block]
        self.copies = [self.send(piece, piece, 17 + d, k.on_first(d)) for d in range(1, 8)]
        self.last = [self.send(piece, piece, 25, k.on_core())]

    def forward(self):
        k = self.peers
        for d in range(1, 8):
            self.copies[d - 1].wait()
            piece = self.full.at[self.rows(k.core, lax.rem(k.p + 8 - d, 8))]
            self.last.append(self.send(piece, piece, 25 + d, k.on_core()))

    def finish(self):
        for copy in self.last:
            copy.wait()


def reduce_kernel(factor, tok_hbm, cot_hbm, gain_ref, w_hbm, gq_ref, terms, mine,
                  gt_ref, oq_ref, oo_ref, og_ref,
                  part, ysum, youter, sums, osum, xin, acc, gkv, grad_normed,
                  tok_ref, cot_ref, w_ref, lsem, tsem, usem, *rest):
    width = gq_ref.shape[1]
    n = width // 128
    g = Grid()
    core = g.core
    middle = 16 * UNIT
    groups = [
        Reduction(Peers(0), UNIT, mine.at[pl.ds(0, middle)], *rest[:10]),
        Reduction(Peers(1), UNIT, mine.at[pl.ds(middle, middle)], *rest[10:]),
    ]

    barrier = pltpu.get_barrier_semaphore()
    k = groups[0].peers
    targets = [k.on_core()] + [k.on_x(d) for d in range(1, 4)]
    targets += [k.on_first(d) for d in range(1, 8)] + [k.on_second(d) for d in range(1, 8)]
    for target in targets:
        pl.semaphore_signal(barrier, inc=1, device_id=target, device_id_type=MESH)
    g.greet(barrier)
    loads = [
        pltpu.make_async_copy(src, dst, lsem.at[i])
        for i, (src, dst) in enumerate(((tok_hbm, tok_ref), (cot_hbm, cot_ref), (w_hbm, w_ref)))
    ]
    for load in loads:
        load.start()
    g.meet(barrier, len(targets))

    def copy(src, dst, slot, target):
        return remote(src, dst, tsem, usem, slot, target)

    outer_before = both(g.has_outer, g.has_before)
    outer_after = both(g.has_outer, g.has_after)
    outer_down = copy(terms.at[2 * core], youter.at[0], 0, g.before)
    outer_up = copy(terms.at[6 + 2 * core], youter.at[1], 1, g.after)
    groups[0].start_core()
    pl.when(outer_before)(outer_down.start)
    pl.when(outer_after)(outer_up.start)
    groups[1].start_core()
    to_partner = {}
    for a in (0, 2, 1):
        to_partner[a] = copy(terms.at[3 * a + 2 * (1 - core)], part.at[a], 2 + a, g.partner)
        to_partner[a].start()
    for load in loads:
        load.wait()
    grad_normed[...] = dot_general(gq_ref[...], w_ref[:, :width], 1, 1)
    for group in groups:
        group.start_scatter()

    to_partner[0].wait()
    sums[0] = (terms[1].astype(F32) + part[0].astype(F32)).astype(BF16)
    down = copy(sums.at[0], ysum.at[0], 5, g.before)
    pl.when(g.has_before)(down.start)
    to_partner[2].wait()
    sums[1] = (terms[7].astype(F32) + part[2].astype(F32)).astype(BF16)
    up = copy(sums.at[1], ysum.at[1], 6, g.after)
    pl.when(g.has_after)(up.start)
    to_partner[1].wait()
    for group in groups:
        group.start_second()

    outward = copy(osum, xin, 7, g.outer)

    @pl.when(g.has_outer)
    def _():
        acc[...] = terms[3 + 2 * core].astype(F32)

        @pl.when(g.has_after)
        def _():
            outer_down.wait_recv()
            acc[...] += youter[0].astype(F32)

        @pl.when(g.has_before)
        def _():
            outer_up.wait_recv()
            acc[...] += youter[1].astype(F32)

        osum[...] = acc[...].astype(BF16)
        outward.start()

    for group in groups:
        group.start_x()
    for group in groups:
        group.start_gather()
    acc[...] = terms[4].astype(F32) + part[1].astype(F32)

    @pl.when(g.has_after)
    def _():
        down.wait_recv()
        acc[...] += ysum[0].astype(F32)

    @pl.when(g.has_before)
    def _():
        up.wait_recv()
        acc[...] += ysum[1].astype(F32)

    @pl.when(g.has_outer)
    def _():
        outward.wait()
        acc[...] += xin[...].astype(F32)

    gkv[...] = acc[...].astype(BF16)
    gain = gain_ref[...]
    _, centred, inverse = norm_parts(tok_ref[...])
    scaled = (grad_normed[...] + dot_general(gkv[...], w_ref[:, width:], 1, 1)) * gain
    inner = inverse * (
        scaled
        - jnp.mean(scaled, -1, keepdims=True)
        - centred * jnp.mean(scaled * centred, -1, keepdims=True)
    )
    gt_ref[...] = (cot_ref[...].astype(F32) + inner).astype(BF16)
    for group in groups:
        group.forward()
    products = jnp.zeros((width, 128), F32)
    for half, group in enumerate(groups):
        group.finish()
        for c in range(2 * n):
            place_at = half * 2 * n + c
            value = group.full[c * width:(c + 1) * width, :].astype(F32) * factor
            if place_at < 3 * n:
                lanes = slice(place_at * 128, (place_at + 1) * 128)
                oq_ref[:, lanes] = value
                products += value * w_ref[:, lanes].astype(F32)
            else:
                oo_ref[:, (place_at - 3 * n) * 128:(place_at - 3 * n + 1) * 128] = value
    total = jnp.broadcast_to(jnp.sum(products, -1, keepdims=True), (width, 128)).T
    og_ref[...] = total[:8, :] / gain
    pl.when(outer_before)(outer_down.wait_send)
    pl.when(outer_after)(outer_up.wait_send)
    pl.when(g.has_before)(down.wait_send)
    pl.when(g.has_after)(up.wait_send)


def reduce(factor, tokens, cotangent, gain, weight, grad_q, terms, mine):
    count, width = tokens.shape
    tile = (count, 2 * width)

    def body(*refs):
        reduce_kernel(factor, *refs)

    return pl.pallas_call(
        body,
        out_shape=(
            jax.ShapeDtypeStruct((count, width), BF16),
            jax.ShapeDtypeStruct((width, 3 * width), F32),
            jax.ShapeDtypeStruct((width, width), F32),
            jax.ShapeDtypeStruct((8, width), F32),
        ),
        in_specs=[HBM, HBM, VMEM, HBM] + [VMEM] * 3,
        out_specs=(VMEM,) * 4,
        scratch_shapes=[
            pltpu.VMEM((3,) + tile, BF16),
            pltpu.VMEM((2,) + tile, BF16),
            pltpu.VMEM((2,) + tile, BF16),
            pltpu.VMEM((2,) + tile, BF16),
            pltpu.VMEM(tile, BF16),
            pltpu.VMEM(tile, BF16),
            pltpu.VMEM(tile, F32),
            pltpu.VMEM(tile, BF16),
            pltpu.VMEM((count, width), F32),
            pltpu.VMEM((count, width), BF16),
            pltpu.VMEM((count, width), BF16),
            pltpu.VMEM((width, 3 * width), BF16),
            pltpu.SemaphoreType.DMA((3,)),
            pltpu.SemaphoreType.DMA((8,)),
            pltpu.SemaphoreType.DMA((8,)),
        ] + Reduction.scratch(UNIT) * 2,
        compiler_params=pltpu.CompilerParams(
            collective_id=0, has_side_effects=True, vmem_limit_bytes=LIMIT
        ),
        name="key_terms_and_all_reduce",
    )(tokens, cotangent, gain, weight, grad_q, terms, mine)


def on_device(tokens, cotangent, key_blocks, qkv_weight, out_weight, norm_gain):
    width = tokens.shape[-1]
    rows = tokens.reshape(-1, width)
    count = rows.shape[0]
    gain = norm_gain.reshape(1, width)
    cot_rows = cotangent.reshape(-1, width)
    block_list = key_blocks.reshape(key_blocks.shape[2], key_blocks.shape[3])
    blocks = block_list.shape[0]
    queries, grad_attended, neighbourhood, normed = project(
        rows, cot_rows, gain, qkv_weight, out_weight
    )
    grad_queries, key_terms, layer_rows, mine = attention(
        block_list, queries, grad_attended,
        neighbourhood.reshape(9 * blocks, count // blocks, 2 * width), normed,
        rows, cot_rows, out_weight,
    )
    factor = 1.0 / math.sqrt(count * lax.axis_size("tm") * lax.axis_size("height"))
    grad_tokens, grad_qkv, grad_out, grad_gain = reduce(
        factor, rows, cot_rows, gain, qkv_weight, grad_queries,
        key_terms.reshape(9, count, 2 * width), mine,
    )
    return (
        layer_rows.reshape(tokens.shape),
        grad_tokens.reshape(tokens.shape),
        grad_qkv,
        grad_out,
        grad_gain[0],
    )


def solution(mesh):
    split = P("tm", "height", None, None)
    return jax.shard_map(
        on_device, mesh=mesh,
        in_specs=(split, split, split, P(), P(), P()),
        out_specs=(split, split, P(), P(), P()),
        check_vma=False,
    )
```

```python
import math

import jax
import jax.numpy as jnp
from jax import lax
from jax.experimental import pallas as pl
from jax.experimental.pallas import tpu as pltpu
from jax.sharding import PartitionSpec as P

HEADS = 6
EPSILON = 1e-05
F32 = jnp.float32
BF16 = jnp.bfloat16
MESH = pl.DeviceIdType.MESH
UNIT = 80
LIMIT = 28 << 20
VMEM = pl.BlockSpec(memory_space=pltpu.VMEM)
HBM = pl.BlockSpec(memory_space=pltpu.HBM)


def norm_parts(token_rows):
    values_in = token_rows.astype(F32)
    center = jnp.mean(values_in, -1, keepdims=True)
    spread = jnp.mean(jnp.square(values_in - center), -1, keepdims=True)
    inverse_scale = lax.rsqrt(spread + EPSILON)
    centred = (values_in - center) * inverse_scale
    return values_in, centred, inverse_scale


def dot_general(a, b, ca, cb):
    return lax.dot_general(a, b, (((ca,), (cb,)), ((), ())), preferred_element_type=F32)


def attention_kernel(list_ref, q_ref, ga_ref, nb_ref, normed_ref, tok_hbm, cot_hbm, ow_hbm,
                     gq_ref, terms_ref, lo_ref, mine_ref,
                     acc, kv, att_ref, grads, tok_ref, cot_ref, ow_ref, sem):
    loads = [
        pltpu.make_async_copy(src, dst, sem.at[i])
        for i, (src, dst) in enumerate(((tok_hbm, tok_ref), (cot_hbm, cot_ref), (ow_hbm, ow_ref)))
    ]
    for load in loads:
        load.start()
    blocks, length = list_ref.shape
    rows = nb_ref.shape[1]
    width = q_ref.shape[1]
    scale = 1.0 / math.sqrt(width // HEADS)
    acc[...] = jnp.zeros_like(acc)
    first = lax.broadcasted_iota(jnp.int32, (rows, 128), 1) < 64
    zero = jnp.zeros((rows, 128), BF16)

    def split(pair):
        return jnp.concatenate([jnp.where(first, pair, zero), jnp.where(first, zero, pair)], 0)

    def join(both):
        return jnp.where(first, both[:rows], both[rows:])

    def body(n, carry):
        at = pl.multiple_of(n * rows, rows)
        for j in range(length):
            kv[j * rows:(j + 1) * rows, :] = nb_ref[list_ref[n, j]]
        for p in range(width // 128):
            lanes = slice(p * 128, (p + 1) * 128)
            vlanes = slice(width + p * 128, width + (p + 1) * 128)
            qs = split(q_ref[pl.ds(at, rows), lanes] * BF16(scale))
            gs = split(ga_ref[pl.ds(at, rows), lanes])
            keys = kv[:, lanes]
            values = kv[:, vlanes]
            scores = dot_general(keys, qs, 1, 1)
            top = jnp.max(scores, 0, keepdims=True)
            raw = jnp.exp(scores - top)
            full = raw * (1.0 / jnp.sum(raw, 0, keepdims=True))
            low = full.astype(BF16)
            att_ref[pl.ds(at, rows), lanes] = join(dot_general(low, values, 0, 0)).astype(BF16)
            probs = dot_general(values, gs, 1, 1)
            dots = jnp.sum(full * probs, 0, keepdims=True)
            grad = (full * (probs - dots)).astype(BF16)
            gq_ref[pl.ds(at, rows), lanes] = (join(dot_general(grad, keys, 0, 0)) * scale).astype(BF16)
            gk = dot_general(grad, qs, 1, 0)
            gv = dot_general(low, gs, 1, 0)
            for j in range(length):
                b = list_ref[n, j]
                part = slice(j * rows, (j + 1) * rows)
                acc[b, :, lanes] = acc[b, :, lanes] + gk[part]
                acc[b, :, vlanes] = acc[b, :, vlanes] + gv[part]
        return carry

    lax.fori_loop(0, blocks, body, 0)
    terms_ref[...] = acc[...].astype(BF16)
    n = width // 128
    tile = blocks * rows
    grads[...] = jnp.zeros_like(grads)

    def add_tile(i, carry):
        normed_t = normed_ref[i].T
        keys = terms_ref[pl.ds(i * blocks, blocks)].reshape(tile, 2 * width)
        grads[...] += dot_general(normed_t, keys, 1, 0)
        return carry

    lax.fori_loop(0, 9, add_tile, 0)
    normed_t = normed_ref[4].T
    for load in loads:
        load.wait()
    att_t = att_ref[...].T
    for c in range(n):
        lanes = slice(c * 128, (c + 1) * 128)
        mine_ref[c * width:(c + 1) * width, :] = dot_general(
            normed_t, gq_ref[:, lanes], 1, 0).astype(BF16)
        mine_ref[(3 * n + c) * width:(3 * n + c + 1) * width, :] = dot_general(
            att_t, cot_ref[:, lanes], 1, 0).astype(BF16)
    for c in range(2 * n):
        mine_ref[(n + c) * width:(n + c + 1) * width, :] = grads[:, c * 128:(c + 1) * 128].astype(BF16)
    done = 4 * n * width
    mine_ref[done:, :] = jnp.zeros((64 * UNIT - done, 128), BF16)
    out = dot_general(att_ref[...], ow_ref[...], 1, 0)
    lo_ref[...] = (tok_ref[...].astype(F32) + out).astype(BF16)


def attention(block_list, queries, grad_attended, neighbourhood, normed, tokens, cotangent, out_weight):
    count, width = queries.shape
    blocks = block_list.shape[0]
    rows = count // blocks
    return pl.pallas_call(
        attention_kernel,
        out_shape=(
            jax.ShapeDtypeStruct((count, width), BF16),
            jax.ShapeDtypeStruct((9 * blocks, rows, 2 * width), BF16),
            jax.ShapeDtypeStruct((count, width), BF16),
            jax.ShapeDtypeStruct((64 * UNIT, 128), BF16),
        ),
        in_specs=[pl.BlockSpec(memory_space=pltpu.SMEM)] + [VMEM] * 4 + [HBM] * 3,
        out_specs=(VMEM,) * 4,
        scratch_shapes=[
            pltpu.VMEM((9 * blocks, rows, 2 * width), F32),
            pltpu.VMEM((block_list.shape[1] * rows, 2 * width), BF16),
            pltpu.VMEM((count, width), BF16),
            pltpu.VMEM((width, 2 * width), F32),
            pltpu.VMEM((count, width), BF16),
            pltpu.VMEM((count, width), BF16),
            pltpu.VMEM((width, width), BF16),
            pltpu.SemaphoreType.DMA((3,)),
        ],
        compiler_params=pltpu.CompilerParams(vmem_limit_bytes=LIMIT),
        name="sparse_attention",
    )(block_list, queries, grad_attended, neighbourhood, normed, tokens, cotangent, out_weight)


def place():
    t = lax.axis_index("tm")
    h = lax.axis_index("height")
    return t // 8, lax.rem(t, 8), h // 4, lax.rem(h // 2, 2), lax.rem(h, 2)


def device(x, y, z, core):
    return ((x // 2) * 8 + y, z * 4 + lax.rem(x, 2) * 2 + core)


class Grid:
    def __init__(self):
        self.t = lax.axis_index("tm")
        self.h = lax.axis_index("height")
        self.core = lax.rem(self.h, 2)
        step = 2 * self.core - 1
        self.partner = (self.t, self.h - step)
        self.outer = (self.t, self.h + step)
        self.before = (self.t - 1, self.h)
        self.after = (self.t + 1, self.h)
        top = lax.axis_size("height") - 1
        self.has_outer = jnp.logical_and(self.h + step >= 0, self.h + step <= top)
        self.has_before = self.t > 0
        self.has_after = self.t < lax.axis_size("tm") - 1

    def greet(self, barrier):
        for there, target in ((self.has_outer, self.outer), (self.has_before, self.before),
                              (self.has_after, self.after)):
            @pl.when(there)
            def _():
                pl.semaphore_signal(barrier, inc=1, device_id=target, device_id_type=MESH)

    def meet(self, barrier, peers):
        number = jnp.int32(peers)
        for there in (self.has_outer, self.has_before, self.has_after):
            number += there.astype(jnp.int32)
        pl.semaphore_wait(barrier, number)


def remote(src, dst, ssem, rsem, slot, target):
    return pltpu.make_async_remote_copy(
        src_ref=src, dst_ref=dst, send_sem=ssem.at[slot], recv_sem=rsem.at[slot],
        device_id=target, device_id_type=MESH,
    )


def both(a, b):
    return jnp.logical_and(a, b)


def project_kernel(tok_hbm, cot_hbm, gain_ref, w_hbm, ow_hbm, q_ref, ga_ref, nb, normed_ref,
                   tiles, cot_ref, w_ref, ow_ref, lsem, ssem, rsem):
    width = q_ref.shape[1]
    g = Grid()
    core = g.core
    barrier = pltpu.get_barrier_semaphore()
    pl.semaphore_signal(barrier, inc=1, device_id=g.partner, device_id_type=MESH)
    g.greet(barrier)
    loads = [
        pltpu.make_async_copy(src, dst, lsem.at[i])
        for i, (src, dst) in enumerate(
            ((tok_hbm, tiles.at[4]), (w_hbm, w_ref), (cot_hbm, cot_ref), (ow_hbm, ow_ref)))
    ]
    for load in loads:
        load.start()
    g.meet(barrier, 1)

    far = 3 + 2 * core
    near = 3 + 2 * (1 - core)

    def copy(src, dst, slot, target):
        return remote(src, tiles.at[dst], ssem, rsem, slot, target)

    to_outer = copy(tok_hbm, near, 1, g.outer)
    up = copy(tok_hbm, 1, 2, g.after)
    down = copy(tok_hbm, 7, 3, g.before)
    to_partner = copy(tok_hbm, far, 0, g.partner)
    up_outer = copy(tiles.at[far], 2 * core, 4, g.after)
    down_outer = copy(tiles.at[far], 6 + 2 * core, 5, g.before)
    low_partner = copy(tiles.at[1], 2 * core, 6, g.partner)
    high_partner = copy(tiles.at[7], 6 + 2 * core, 7, g.partner)
    outer_before = both(g.has_outer, g.has_before)
    outer_after = both(g.has_outer, g.has_after)

    pl.when(g.has_outer)(to_outer.start)
    pl.when(g.has_after)(up.start)
    pl.when(g.has_before)(down.start)
    to_partner.start()

    def fill(slot):
        _, centred, _ = norm_parts(tiles[slot])
        normed = (centred * gain_ref[...]).astype(BF16)
        normed_ref[slot] = normed
        nb[slot] = dot_general(normed, w_ref[:, width:], 1, 0).astype(BF16)
        return normed

    def fill_if(there, slot):
        @pl.when(there)
        def _():
            fill(slot)

        @pl.when(jnp.logical_not(there))
        def _():
            normed_ref[slot] = jnp.zeros_like(normed_ref[slot])

    for load in loads:
        load.wait()
    normed = fill(4)
    q_ref[...] = dot_general(normed, w_ref[:, :width], 1, 0).astype(BF16)
    ga_ref[...] = dot_general(cot_ref[...], ow_ref[...], 1, 1).astype(BF16)
    pl.when(g.has_outer)(to_outer.wait)
    pl.when(outer_after)(up_outer.start)
    pl.when(outer_before)(down_outer.start)

    @pl.when(g.has_before)
    def _():
        up.wait_recv()
        low_partner.start()

    @pl.when(g.has_after)
    def _():
        down.wait_recv()
        high_partner.start()

    to_partner.wait()
    fill(near)
    fill_if(g.has_outer, far)
    fill_if(g.has_before, 1)
    fill_if(g.has_after, 7)
    pl.when(g.has_before)(low_partner.wait)
    fill_if(g.has_before, 2 * (1 - core))
    pl.when(g.has_after)(high_partner.wait)
    fill_if(g.has_after, 6 + 2 * (1 - core))
    pl.when(outer_before)(up_outer.wait_recv)
    fill_if(outer_before, 2 * core)
    pl.when(outer_after)(down_outer.wait_recv)
    fill_if(outer_after, 6 + 2 * core)
    pl.when(g.has_after)(up.wait_send)
    pl.when(g.has_before)(down.wait_send)
    pl.when(outer_after)(up_outer.wait_send)
    pl.when(outer_before)(down_outer.wait_send)


def project(tokens, cotangent, gain, weight, out_weight):
    count, width = tokens.shape
    return pl.pallas_call(
        project_kernel,
        out_shape=(
            jax.ShapeDtypeStruct((count, width), BF16),
            jax.ShapeDtypeStruct((count, width), BF16),
            jax.ShapeDtypeStruct((9, count, 2 * width), BF16),
            jax.ShapeDtypeStruct((9, count, width), BF16),
        ),
        in_specs=[HBM, HBM, VMEM, HBM, HBM],
        out_specs=(VMEM,) * 4,
        scratch_shapes=[
            pltpu.VMEM((9, count, width), BF16),
            pltpu.VMEM((count, width), BF16),
            pltpu.VMEM((width, 3 * width), BF16),
            pltpu.VMEM((width, width), BF16),
            pltpu.SemaphoreType.DMA((4,)),
            pltpu.SemaphoreType.DMA((8,)),
            pltpu.SemaphoreType.DMA((8,)),
        ],
        compiler_params=pltpu.CompilerParams(
            collective_id=1, has_side_effects=True, vmem_limit_bytes=LIMIT
        ),
        name="halo_and_project",
    )(tokens, cotangent, gain, weight, out_weight)


class Peers:
    def __init__(self):
        x_hi, self.y, self.z, x_lo, self.core = place()
        self.x = x_hi * 2 + x_lo
        self.along_z = self.core == 0
        self.p = jnp.where(self.along_z, self.z, self.y)
        self.q = jnp.where(self.along_z, self.y, self.z)

    def on_core(self):
        return device(self.x, self.y, self.z, 1 - self.core)

    def on_x(self, d):
        return device(lax.rem(self.x + d, 4), self.y, self.z, self.core)

    def on_first(self, d):
        there = lax.rem(self.p + d, 8)
        return device(self.x, jnp.where(self.along_z, self.y, there),
                      jnp.where(self.along_z, there, self.z), self.core)

    def on_second(self, d):
        there = lax.rem(self.q + d, 8)
        return device(self.x, jnp.where(self.along_z, there, self.y),
                      jnp.where(self.along_z, self.z, there), self.core)


class Reduction:
    def __init__(self, mine, rc, s1, r1, s2, r2, s3, r3, full, ssem, rsem):
        self.peers, self.quarter, self.half = Peers(), 8 * UNIT, 32 * UNIT
        self.mine, self.rc, self.s1, self.r1, self.s2, self.r2 = mine, rc, s1, r1, s2, r2
        self.s3, self.r3, self.full, self.ssem, self.rsem = s3, r3, full, ssem, rsem

    @staticmethod
    def scratch():
        half = 32 * UNIT
        return [
            pltpu.VMEM((half, 128), BF16),
            pltpu.VMEM((half, 128), BF16),
            pltpu.VMEM((3, half // 4, 128), BF16),
            pltpu.VMEM((half // 4, 128), BF16),
            pltpu.VMEM((7, UNIT, 128), BF16),
            pltpu.VMEM((UNIT, 128), BF16),
            pltpu.VMEM((8, UNIT, 128), BF16),
            pltpu.SemaphoreType.DMA((35,)),
            pltpu.SemaphoreType.DMA((35,)),
        ]

    def send(self, src, dst, slot, target):
        copy = remote(src, dst, self.ssem, self.rsem, slot, target)
        copy.start()
        return copy

    def rows(self, core, x):
        return pl.ds(pl.multiple_of(core * self.half + x * self.quarter, self.quarter), self.quarter)

    def start_core(self):
        k = self.peers
        self.copies = []
        for d in (1, 2, 3, 4):
            x = lax.rem(k.x + d, 4)
            self.copies.append(self.send(
                self.mine.at[self.rows(1 - k.core, x)], self.rc.at[self.rows(0, x)], d - 1, k.on_core()))

    def start_x(self):
        k = self.peers
        arrived = self.copies
        self.copies = []
        for d in (1, 2, 3, 4):
            arrived[d - 1].wait()
            x = lax.rem(k.x + d, 4)
            own = self.mine[self.rows(k.core, x), :].astype(F32)
            block = self.rows(0, x)
            self.s1[block, :] = (own + self.rc[block, :].astype(F32)).astype(BF16)
            if d < 4:
                self.copies.append(self.send(self.s1.at[block], self.r1.at[d - 1], 3 + d, k.on_x(d)))

    def start_first(self):
        k = self.peers
        total = self.s1[self.rows(0, k.x), :].astype(F32)
        for d in range(1, 4):
            self.copies[d - 1].wait()
            total += self.r1[d - 1].astype(F32)
        self.s2[...] = total.astype(BF16)
        self.copies = []
        for d in range(1, 8):
            block = pl.ds(pl.multiple_of(lax.rem(k.p + d, 8) * UNIT, UNIT), UNIT)
            self.copies.append(self.send(self.s2.at[block], self.r2.at[d - 1], 6 + d, k.on_first(d)))

    def start_second(self):
        k = self.peers
        total = self.s2[pl.ds(pl.multiple_of(k.p * UNIT, UNIT), UNIT), :].astype(F32)
        for d in range(1, 8):
            self.copies[d - 1].wait()
            total += self.r2[d - 1].astype(F32)
        self.s3[...] = total.astype(BF16)
        self.copies = [self.send(self.s3, self.r3.at[k.q], 13 + d, k.on_second(d)) for d in range(1, 8)]
        self.r3[k.q] = self.s3[...]

    def start_gather(self):
        k = self.peers
        for copy in self.copies:
            copy.wait()
        total = self.r3[0].astype(F32)
        for i in range(1, 8):
            total += self.r3[i].astype(F32)
        start = k.core * self.half + k.x * self.quarter + k.p * UNIT
        block = pl.ds(pl.multiple_of(start, UNIT), UNIT)
        self.full[block, :] = total.astype(BF16)
        piece = self.full.at[block]
        self.copies = [self.send(piece, piece, 20 + d, k.on_first(d)) for d in range(1, 8)]

    def gather_x(self):
        k = self.peers
        for copy in self.copies:
            copy.wait()
        piece = self.full.at[self.rows(k.core, k.x)]
        self.copies = [self.send(piece, piece, 27 + d, k.on_x(d)) for d in range(1, 4)]
        self.last = [self.send(piece, piece, 31, k.on_core())]

    def finish(self):
        k = self.peers
        for d in range(1, 4):
            self.copies[d - 1].wait()
            piece = self.full.at[self.rows(k.core, lax.rem(k.x + 4 - d, 4))]
            self.last.append(self.send(piece, piece, 31 + d, k.on_core()))
        for copy in self.last:
            copy.wait()


def reduce_kernel(tok_hbm, cot_hbm, gain_ref, w_hbm, gq_ref, terms, mine,
                  gt_ref, full,
                  part, ysum, youter, sums, osum, xin, acc, gkv, grad_normed,
                  tok_ref, cot_ref, w_ref, lsem, tsem, usem, *rest):
    width = gq_ref.shape[1]
    g = Grid()
    core = g.core
    group = Reduction(mine, *rest[:7], full, *rest[7:])

    barrier = pltpu.get_barrier_semaphore()
    k = group.peers
    targets = [k.on_core()] + [k.on_x(d) for d in range(1, 4)]
    targets += [k.on_first(d) for d in range(1, 8)] + [k.on_second(d) for d in range(1, 8)]
    for target in targets:
        pl.semaphore_signal(barrier, inc=1, device_id=target, device_id_type=MESH)
    g.greet(barrier)
    loads = [
        pltpu.make_async_copy(src, dst, lsem.at[i])
        for i, (src, dst) in enumerate(((tok_hbm, tok_ref), (cot_hbm, cot_ref), (w_hbm, w_ref)))
    ]
    for load in loads:
        load.start()
    g.meet(barrier, len(targets))

    def copy(src, dst, slot, target):
        return remote(src, dst, tsem, usem, slot, target)

    outer_before = both(g.has_outer, g.has_before)
    outer_after = both(g.has_outer, g.has_after)
    outer_down = copy(terms.at[2 * core], youter.at[0], 0, g.before)
    outer_up = copy(terms.at[6 + 2 * core], youter.at[1], 1, g.after)
    group.start_core()
    pl.when(outer_before)(outer_down.start)
    pl.when(outer_after)(outer_up.start)
    to_partner = {}
    for a in (0, 2, 1):
        to_partner[a] = copy(terms.at[3 * a + 2 * (1 - core)], part.at[a], 2 + a, g.partner)
        to_partner[a].start()
    group.start_x()
    for load in loads:
        load.wait()
    to_partner[0].wait()
    sums[0] = (terms[1].astype(F32) + part[0].astype(F32)).astype(BF16)
    down = copy(sums.at[0], ysum.at[0], 5, g.before)
    pl.when(g.has_before)(down.start)
    to_partner[2].wait()
    sums[1] = (terms[7].astype(F32) + part[2].astype(F32)).astype(BF16)
    up = copy(sums.at[1], ysum.at[1], 6, g.after)
    pl.when(g.has_after)(up.start)
    to_partner[1].wait()
    grad_normed[...] = dot_general(gq_ref[...], w_ref[:, :width], 1, 1)
    group.start_first()

    outward = copy(osum, xin, 7, g.outer)

    @pl.when(g.has_outer)
    def _():
        acc[...] = terms[3 + 2 * core].astype(F32)

        @pl.when(g.has_after)
        def _():
            outer_down.wait_recv()
            acc[...] += youter[0].astype(F32)

        @pl.when(g.has_before)
        def _():
            outer_up.wait_recv()
            acc[...] += youter[1].astype(F32)

        osum[...] = acc[...].astype(BF16)
        outward.start()

    group.start_second()
    group.start_gather()
    acc[...] = terms[4].astype(F32) + part[1].astype(F32)

    @pl.when(g.has_after)
    def _():
        down.wait_recv()
        acc[...] += ysum[0].astype(F32)

    @pl.when(g.has_before)
    def _():
        up.wait_recv()
        acc[...] += ysum[1].astype(F32)

    @pl.when(g.has_outer)
    def _():
        outward.wait()
        acc[...] += xin[...].astype(F32)

    gkv[...] = acc[...].astype(BF16)
    group.gather_x()
    gain = gain_ref[...]
    _, centred, inverse = norm_parts(tok_ref[...])
    scaled = (grad_normed[...] + dot_general(gkv[...], w_ref[:, width:], 1, 1)) * gain
    inner = inverse * (
        scaled
        - jnp.mean(scaled, -1, keepdims=True)
        - centred * jnp.mean(scaled * centred, -1, keepdims=True)
    )
    gt_ref[...] = (cot_ref[...].astype(F32) + inner).astype(BF16)
    group.finish()
    pl.when(outer_before)(outer_down.wait_send)
    pl.when(outer_after)(outer_up.wait_send)
    pl.when(g.has_before)(down.wait_send)
    pl.when(g.has_after)(up.wait_send)


def finish_kernel(factor, full, w_ref, gain_ref, oq_ref, oo_ref, og_ref):
    width = oo_ref.shape[0]
    n = width // 128
    products = jnp.zeros((width, 128), F32)
    for c in range(4 * n):
        value = full[c * width:(c + 1) * width, :].astype(F32) * factor
        if c < 3 * n:
            lanes = slice(c * 128, (c + 1) * 128)
            oq_ref[:, lanes] = value
            products += value * w_ref[:, lanes].astype(F32)
        else:
            oo_ref[:, (c - 3 * n) * 128:(c - 3 * n + 1) * 128] = value
    total = jnp.broadcast_to(jnp.sum(products, -1, keepdims=True), (width, 128)).T
    og_ref[...] = total[:1, :] / gain_ref[...]


def finish(factor, full, weight, gain):
    width = gain.shape[1]

    def body(*refs):
        finish_kernel(factor, *refs)

    return pl.pallas_call(
        body,
        out_shape=(
            jax.ShapeDtypeStruct((width, 3 * width), F32),
            jax.ShapeDtypeStruct((width, width), F32),
            jax.ShapeDtypeStruct((1, width), F32),
        ),
        in_specs=[VMEM] * 3,
        out_specs=(VMEM,) * 3,
        compiler_params=pltpu.CompilerParams(vmem_limit_bytes=LIMIT),
        name="scale_weight_grads",
    )(full, weight, gain)


def reduce(tokens, cotangent, gain, weight, grad_q, terms, mine):
    count, width = tokens.shape
    tile = (count, 2 * width)
    return pl.pallas_call(
        reduce_kernel,
        out_shape=(
            jax.ShapeDtypeStruct((count, width), BF16),
            jax.ShapeDtypeStruct((64 * UNIT, 128), BF16),
        ),
        in_specs=[HBM, HBM, VMEM, HBM] + [VMEM] * 3,
        out_specs=(VMEM,) * 2,
        scratch_shapes=[
            pltpu.VMEM((3,) + tile, BF16),
            pltpu.VMEM((2,) + tile, BF16),
            pltpu.VMEM((2,) + tile, BF16),
            pltpu.VMEM((2,) + tile, BF16),
            pltpu.VMEM(tile, BF16),
            pltpu.VMEM(tile, BF16),
            pltpu.VMEM(tile, F32),
            pltpu.VMEM(tile, BF16),
            pltpu.VMEM((count, width), F32),
            pltpu.VMEM((count, width), BF16),
            pltpu.VMEM((count, width), BF16),
            pltpu.VMEM((width, 3 * width), BF16),
            pltpu.SemaphoreType.DMA((3,)),
            pltpu.SemaphoreType.DMA((8,)),
            pltpu.SemaphoreType.DMA((8,)),
        ] + Reduction.scratch(),
        compiler_params=pltpu.CompilerParams(
            collective_id=0, has_side_effects=True, vmem_limit_bytes=LIMIT
        ),
        name="key_terms_and_all_reduce",
    )(tokens, cotangent, gain, weight, grad_q, terms, mine)


def on_device(tokens, cotangent, key_blocks, qkv_weight, out_weight, norm_gain):
    width = tokens.shape[-1]
    rows = tokens.reshape(-1, width)
    count = rows.shape[0]
    gain = norm_gain.reshape(1, width)
    cot_rows = cotangent.reshape(-1, width)
    block_list = key_blocks.reshape(key_blocks.shape[2], key_blocks.shape[3])
    blocks = block_list.shape[0]
    rows, cot_rows, qkv_weight, out_weight = (
        pltpu.with_memory_space_constraint(a, pltpu.HBM)
        for a in (rows, cot_rows, qkv_weight, out_weight)
    )
    queries, grad_attended, neighbourhood, normed = project(
        rows, cot_rows, gain, qkv_weight, out_weight
    )
    grad_queries, key_terms, layer_rows, mine = attention(
        block_list, queries, grad_attended,
        neighbourhood.reshape(9 * blocks, count // blocks, 2 * width), normed,
        rows, cot_rows, out_weight,
    )
    factor = 1.0 / math.sqrt(count * lax.axis_size("tm") * lax.axis_size("height"))
    grad_tokens, full = reduce(
        rows, cot_rows, gain, qkv_weight, grad_queries,
        key_terms.reshape(9, count, 2 * width), mine,
    )
    grad_qkv, grad_out, grad_gain = finish(factor, full, qkv_weight, gain)
    return (
        layer_rows.reshape(tokens.shape),
        grad_tokens.reshape(tokens.shape),
        grad_qkv,
        grad_out,
        grad_gain[0],
    )


def solution(mesh):
    split = P("tm", "height", None, None)
    return jax.shard_map(
        on_device, mesh=mesh,
        in_specs=(split, split, split, P(), P(), P()),
        out_specs=(split, split, P(), P(), P()),
        check_vma=False,
    )
```

```python
import math

import jax
import jax.numpy as jnp
from jax import lax
from jax.experimental import pallas as pl
from jax.experimental.pallas import tpu as pltpu
from jax.sharding import PartitionSpec as P

HEADS = 6
EPSILON = 1e-05
F32 = jnp.float32
BF16 = jnp.bfloat16
MESH = pl.DeviceIdType.MESH
UNIT = 144
LIMIT = 28 << 20
VMEM = pl.BlockSpec(memory_space=pltpu.VMEM)
HBM = pl.BlockSpec(memory_space=pltpu.HBM)


def norm_parts(token_rows):
    values_in = token_rows.astype(F32)
    center = jnp.mean(values_in, -1, keepdims=True)
    spread = jnp.mean(jnp.square(values_in - center), -1, keepdims=True)
    inverse_scale = lax.rsqrt(spread + EPSILON)
    centred = (values_in - center) * inverse_scale
    return values_in, centred, inverse_scale


def dot_general(a, b, ca, cb):
    return lax.dot_general(a, b, (((ca,), (cb,)), ((), ())), preferred_element_type=F32)


def attention_kernel(list_ref, q_ref, ga_ref, nb_ref, normed_ref, tok_hbm, cot_hbm, ow_hbm,
                     gq_ref, terms_ref, lo_ref, mine_ref,
                     acc, kv, att_ref, grads, tok_ref, cot_ref, ow_ref, sem):
    loads = [
        pltpu.make_async_copy(src, dst, sem.at[i])
        for i, (src, dst) in enumerate(((tok_hbm, tok_ref), (cot_hbm, cot_ref), (ow_hbm, ow_ref)))
    ]
    for load in loads:
        load.start()
    blocks, length = list_ref.shape
    rows = nb_ref.shape[1]
    width = q_ref.shape[1]
    scale = 1.0 / math.sqrt(width // HEADS)
    acc[...] = jnp.zeros_like(acc)
    first = lax.broadcasted_iota(jnp.int32, (rows, 128), 1) < 64
    zero = jnp.zeros((rows, 128), BF16)

    def split(pair):
        return jnp.concatenate([jnp.where(first, pair, zero), jnp.where(first, zero, pair)], 0)

    def join(both):
        return jnp.where(first, both[:rows], both[rows:])

    def body(n, carry):
        at = pl.multiple_of(n * rows, rows)
        for j in range(length):
            kv[j * rows:(j + 1) * rows, :] = nb_ref[list_ref[n, j]]
        for p in range(width // 128):
            lanes = slice(p * 128, (p + 1) * 128)
            vlanes = slice(width + p * 128, width + (p + 1) * 128)
            qs = split(q_ref[pl.ds(at, rows), lanes] * BF16(scale))
            gs = split(ga_ref[pl.ds(at, rows), lanes])
            keys = kv[:, lanes]
            values = kv[:, vlanes]
            scores = dot_general(keys, qs, 1, 1)
            top = jnp.max(scores, 0, keepdims=True)
            raw = jnp.exp(scores - top)
            full = raw * (1.0 / jnp.sum(raw, 0, keepdims=True))
            low = full.astype(BF16)
            att_ref[pl.ds(at, rows), lanes] = join(dot_general(low, values, 0, 0)).astype(BF16)
            probs = dot_general(values, gs, 1, 1)
            dots = jnp.sum(full * probs, 0, keepdims=True)
            grad = (full * (probs - dots)).astype(BF16)
            gq_ref[pl.ds(at, rows), lanes] = (join(dot_general(grad, keys, 0, 0)) * scale).astype(BF16)
            gk = dot_general(grad, qs, 1, 0)
            gv = dot_general(low, gs, 1, 0)
            for j in range(length):
                b = list_ref[n, j]
                part = slice(j * rows, (j + 1) * rows)
                acc[b, :, lanes] = acc[b, :, lanes] + gk[part]
                acc[b, :, vlanes] = acc[b, :, vlanes] + gv[part]
        return carry

    lax.fori_loop(0, blocks, body, 0)
    terms_ref[...] = acc[...].astype(BF16)
    n = width // 128
    tile = blocks * rows
    grads[...] = jnp.zeros_like(grads)

    def add_tile(i, carry):
        normed_t = normed_ref[i].T
        keys = terms_ref[pl.ds(i * blocks, blocks)].reshape(tile, 2 * width)
        grads[...] += dot_general(normed_t, keys, 1, 0)
        return carry

    lax.fori_loop(0, 9, add_tile, 0)
    normed_t = normed_ref[4].T
    for load in loads:
        load.wait()
    att_t = att_ref[...].T
    for c in range(n):
        lanes = slice(c * 128, (c + 1) * 128)
        mine_ref[c * width:(c + 1) * width, :] = dot_general(
            normed_t, gq_ref[:, lanes], 1, 0).astype(BF16)
        mine_ref[(3 * n + c) * width:(3 * n + c + 1) * width, :] = dot_general(
            att_t, cot_ref[:, lanes], 1, 0).astype(BF16)
    for c in range(2 * n):
        mine_ref[(n + c) * width:(n + c + 1) * width, :] = grads[:, c * 128:(c + 1) * 128].astype(BF16)
    out = dot_general(att_ref[...], ow_ref[...], 1, 0)
    lo_ref[...] = (tok_ref[...].astype(F32) + out).astype(BF16)


def attention(block_list, queries, grad_attended, neighbourhood, normed, tokens, cotangent, out_weight):
    count, width = queries.shape
    blocks = block_list.shape[0]
    rows = count // blocks
    return pl.pallas_call(
        attention_kernel,
        out_shape=(
            jax.ShapeDtypeStruct((count, width), BF16),
            jax.ShapeDtypeStruct((9 * blocks, rows, 2 * width), BF16),
            jax.ShapeDtypeStruct((count, width), BF16),
            jax.ShapeDtypeStruct((4 * width // 128 * width, 128), BF16),
        ),
        in_specs=[pl.BlockSpec(memory_space=pltpu.SMEM)] + [VMEM] * 4 + [HBM] * 3,
        out_specs=(VMEM,) * 4,
        scratch_shapes=[
            pltpu.VMEM((9 * blocks, rows, 2 * width), F32),
            pltpu.VMEM((block_list.shape[1] * rows, 2 * width), BF16),
            pltpu.VMEM((count, width), BF16),
            pltpu.VMEM((width, 2 * width), F32),
            pltpu.VMEM((count, width), BF16),
            pltpu.VMEM((count, width), BF16),
            pltpu.VMEM((width, width), BF16),
            pltpu.SemaphoreType.DMA((3,)),
        ],
        compiler_params=pltpu.CompilerParams(vmem_limit_bytes=LIMIT),
        name="sparse_attention",
    )(block_list, queries, grad_attended, neighbourhood, normed, tokens, cotangent, out_weight)


def place():
    t = lax.axis_index("tm")
    h = lax.axis_index("height")
    return t // 8, lax.rem(t, 8), h // 4, lax.rem(h // 2, 2), lax.rem(h, 2)


def device(x, y, z, core):
    return ((x // 2) * 8 + y, z * 4 + lax.rem(x, 2) * 2 + core)


class Grid:
    def __init__(self):
        self.t = lax.axis_index("tm")
        self.h = lax.axis_index("height")
        self.core = lax.rem(self.h, 2)
        step = 2 * self.core - 1
        self.partner = (self.t, self.h - step)
        self.outer = (self.t, self.h + step)
        self.before = (self.t - 1, self.h)
        self.after = (self.t + 1, self.h)
        top = lax.axis_size("height") - 1
        self.has_outer = jnp.logical_and(self.h + step >= 0, self.h + step <= top)
        self.has_before = self.t > 0
        self.has_after = self.t < lax.axis_size("tm") - 1

    def greet(self, barrier):
        for there, target in ((self.has_outer, self.outer), (self.has_before, self.before),
                              (self.has_after, self.after)):
            @pl.when(there)
            def _():
                pl.semaphore_signal(barrier, inc=1, device_id=target, device_id_type=MESH)

    def meet(self, barrier, peers):
        number = jnp.int32(peers)
        for there in (self.has_outer, self.has_before, self.has_after):
            number += there.astype(jnp.int32)
        pl.semaphore_wait(barrier, number)


def remote(src, dst, ssem, rsem, slot, target):
    return pltpu.make_async_remote_copy(
        src_ref=src, dst_ref=dst, send_sem=ssem.at[slot], recv_sem=rsem.at[slot],
        device_id=target, device_id_type=MESH,
    )


def both(a, b):
    return jnp.logical_and(a, b)


def project_kernel(tok_hbm, cot_hbm, gain_ref, w_hbm, ow_hbm, q_ref, ga_ref, nb, normed_ref,
                   tiles, cot_ref, w_ref, ow_ref, lsem, ssem, rsem):
    width = q_ref.shape[1]
    g = Grid()
    core = g.core
    barrier = pltpu.get_barrier_semaphore()
    pl.semaphore_signal(barrier, inc=1, device_id=g.partner, device_id_type=MESH)
    g.greet(barrier)
    loads = [
        pltpu.make_async_copy(src, dst, lsem.at[i])
        for i, (src, dst) in enumerate(
            ((tok_hbm, tiles.at[4]), (w_hbm, w_ref), (cot_hbm, cot_ref), (ow_hbm, ow_ref)))
    ]
    for load in loads:
        load.start()
    g.meet(barrier, 1)

    far = 3 + 2 * core
    near = 3 + 2 * (1 - core)

    def copy(src, dst, slot, target):
        return remote(src, tiles.at[dst], ssem, rsem, slot, target)

    to_outer = copy(tok_hbm, near, 1, g.outer)
    up = copy(tok_hbm, 1, 2, g.after)
    down = copy(tok_hbm, 7, 3, g.before)
    to_partner = copy(tok_hbm, far, 0, g.partner)
    up_outer = copy(tiles.at[far], 2 * core, 4, g.after)
    down_outer = copy(tiles.at[far], 6 + 2 * core, 5, g.before)
    low_partner = copy(tiles.at[1], 2 * core, 6, g.partner)
    high_partner = copy(tiles.at[7], 6 + 2 * core, 7, g.partner)
    outer_before = both(g.has_outer, g.has_before)
    outer_after = both(g.has_outer, g.has_after)

    pl.when(g.has_outer)(to_outer.start)
    pl.when(g.has_after)(up.start)
    pl.when(g.has_before)(down.start)
    to_partner.start()

    def fill(slot):
        _, centred, _ = norm_parts(tiles[slot])
        normed = (centred * gain_ref[...].reshape(1, -1)).astype(BF16)
        normed_ref[slot] = normed
        nb[slot] = dot_general(normed, w_ref[:, width:], 1, 0).astype(BF16)
        return normed

    def fill_if(there, slot):
        @pl.when(there)
        def _():
            fill(slot)

        @pl.when(jnp.logical_not(there))
        def _():
            normed_ref[slot] = jnp.zeros_like(normed_ref[slot])

    for load in loads:
        load.wait()
    normed = fill(4)
    q_ref[...] = dot_general(normed, w_ref[:, :width], 1, 0).astype(BF16)
    ga_ref[...] = dot_general(cot_ref[...], ow_ref[...], 1, 1).astype(BF16)
    pl.when(g.has_outer)(to_outer.wait)
    pl.when(outer_after)(up_outer.start)
    pl.when(outer_before)(down_outer.start)

    @pl.when(g.has_before)
    def _():
        up.wait_recv()
        low_partner.start()

    @pl.when(g.has_after)
    def _():
        down.wait_recv()
        high_partner.start()

    to_partner.wait()
    fill(near)
    fill_if(g.has_outer, far)
    fill_if(g.has_before, 1)
    fill_if(g.has_after, 7)
    pl.when(g.has_before)(low_partner.wait)
    fill_if(g.has_before, 2 * (1 - core))
    pl.when(g.has_after)(high_partner.wait)
    fill_if(g.has_after, 6 + 2 * (1 - core))
    pl.when(outer_before)(up_outer.wait_recv)
    fill_if(outer_before, 2 * core)
    pl.when(outer_after)(down_outer.wait_recv)
    fill_if(outer_after, 6 + 2 * core)
    pl.when(g.has_after)(up.wait_send)
    pl.when(g.has_before)(down.wait_send)
    pl.when(outer_after)(up_outer.wait_send)
    pl.when(outer_before)(down_outer.wait_send)


def project(tokens, cotangent, gain, weight, out_weight):
    count, width = tokens.shape
    return pl.pallas_call(
        project_kernel,
        out_shape=(
            jax.ShapeDtypeStruct((count, width), BF16),
            jax.ShapeDtypeStruct((count, width), BF16),
            jax.ShapeDtypeStruct((9, count, 2 * width), BF16),
            jax.ShapeDtypeStruct((9, count, width), BF16),
        ),
        in_specs=[HBM, HBM, VMEM, HBM, HBM],
        out_specs=(VMEM,) * 4,
        scratch_shapes=[
            pltpu.VMEM((9, count, width), BF16),
            pltpu.VMEM((count, width), BF16),
            pltpu.VMEM((width, 3 * width), BF16),
            pltpu.VMEM((width, width), BF16),
            pltpu.SemaphoreType.DMA((4,)),
            pltpu.SemaphoreType.DMA((8,)),
            pltpu.SemaphoreType.DMA((8,)),
        ],
        compiler_params=pltpu.CompilerParams(
            collective_id=1, has_side_effects=True, vmem_limit_bytes=LIMIT
        ),
        name="halo_and_project",
    )(tokens, cotangent, gain, weight, out_weight)


class Peers:
    def __init__(self, swap):
        x_hi, self.y, self.z, x_lo, self.core = place()
        self.x = x_hi * 2 + x_lo
        self.along_z = self.core == swap
        self.p = jnp.where(self.along_z, self.z, self.y)
        self.q = jnp.where(self.along_z, self.y, self.z)

    def on_core(self):
        return device(self.x, self.y, self.z, 1 - self.core)

    def on_x(self, d):
        return device(lax.rem(self.x + d, 4), self.y, self.z, self.core)

    def on_first(self, d):
        there = lax.rem(self.p + d, 8)
        return device(self.x, jnp.where(self.along_z, self.y, there),
                      jnp.where(self.along_z, there, self.z), self.core)

    def on_second(self, d):
        there = lax.rem(self.q + d, 8)
        return device(self.x, jnp.where(self.along_z, there, self.y),
                      jnp.where(self.along_z, self.z, there), self.core)


class Reduction:
    def __init__(self, peers, unit, mine, rc, s1, r1, s2, r2, s3, r3, full, ssem, rsem):
        self.peers, self.unit, self.half = peers, unit, 8 * unit
        self.mine, self.rc, self.s1, self.r1, self.s2, self.r2 = mine, rc, s1, r1, s2, r2
        self.s3, self.r3, self.full, self.ssem, self.rsem = s3, r3, full, ssem, rsem

    @staticmethod
    def scratch(unit):
        half = 8 * unit
        return [
            pltpu.VMEM((half, 128), BF16),
            pltpu.VMEM((half, 128), BF16),
            pltpu.VMEM((7, unit, 128), BF16),
            pltpu.VMEM((unit, 128), BF16),
            pltpu.VMEM((8, unit, 128), BF16),
            pltpu.VMEM((unit, 128), BF16),
            pltpu.VMEM((4, unit, 128), BF16),
            pltpu.VMEM((2 * half, 128), BF16),
            pltpu.SemaphoreType.DMA((33,)),
            pltpu.SemaphoreType.DMA((33,)),
        ]

    def send(self, src, dst, slot, target):
        copy = remote(src, dst, self.ssem, self.rsem, slot, target)
        copy.start()
        return copy

    def rows(self, core, p):
        return pl.ds(pl.multiple_of(core * self.half + p * self.unit, 16), self.unit)

    def half_rows(self, core):
        return pl.ds(pl.multiple_of(core * self.half, 16), self.half)

    def start_core(self):
        k = self.peers
        self.copy = self.send(self.mine.at[self.half_rows(1 - k.core)], self.rc, 0, k.on_core())

    def start_scatter(self):
        k = self.peers
        self.copy.wait()
        own = self.mine[self.half_rows(k.core), :].astype(F32)
        self.s1[...] = (own + self.rc[...].astype(F32)).astype(BF16)
        self.copies = [
            self.send(self.s1.at[self.rows(0, lax.rem(k.p + d, 8))], self.r1.at[d - 1], d, k.on_first(d))
            for d in range(1, 8)
        ]

    def start_second(self):
        k = self.peers
        total = self.s1[self.rows(0, k.p), :].astype(F32)
        for d in range(1, 8):
            self.copies[d - 1].wait()
            total += self.r1[d - 1].astype(F32)
        self.s2[...] = total.astype(BF16)
        self.copies = [
            self.send(self.s2, self.r2.at[k.q], 7 + d, k.on_second(d)) for d in range(1, 8)
        ]
        self.r2[k.q] = self.s2[...]

    def start_x(self):
        k = self.peers
        for copy in self.copies:
            copy.wait()
        total = self.r2[0].astype(F32)
        for i in range(1, 8):
            total += self.r2[i].astype(F32)
        self.s3[...] = total.astype(BF16)
        self.copies = [self.send(self.s3, self.r3.at[k.x], 14 + d, k.on_x(d)) for d in range(1, 4)]
        self.r3[k.x] = self.s3[...]

    def start_gather(self):
        k = self.peers
        for copy in self.copies:
            copy.wait()
        total = self.r3[0].astype(F32)
        for i in range(1, 4):
            total += self.r3[i].astype(F32)
        block = self.rows(k.core, k.p)
        self.full[block, :] = total.astype(BF16)
        piece = self.full.at[block]
        self.copies = [self.send(piece, piece, 17 + d, k.on_first(d)) for d in range(1, 8)]
        self.last = [self.send(piece, piece, 25, k.on_core())]

    def forward(self):
        k = self.peers
        for d in range(1, 8):
            self.copies[d - 1].wait()
            piece = self.full.at[self.rows(k.core, lax.rem(k.p + 8 - d, 8))]
            self.last.append(self.send(piece, piece, 25 + d, k.on_core()))

    def finish(self):
        for copy in self.last:
            copy.wait()


def reduce_kernel(factor, tok_hbm, cot_hbm, gain_ref, w_hbm, gq_ref, terms, mine,
                  gt_ref, oq_ref, oo_ref, og_ref,
                  part, ysum, youter, sums, osum, xin, acc, gkv, grad_normed,
                  tok_ref, cot_ref, w_ref, lsem, tsem, usem, *rest):
    width = gq_ref.shape[1]
    n = width // 128
    g = Grid()
    core = g.core
    middle = 16 * UNIT
    groups = [
        Reduction(Peers(0), UNIT, mine.at[pl.ds(0, middle)], *rest[:10]),
        Reduction(Peers(1), UNIT, mine.at[pl.ds(middle, middle)], *rest[10:]),
    ]

    barrier = pltpu.get_barrier_semaphore()
    k = groups[0].peers
    targets = [k.on_core()] + [k.on_x(d) for d in range(1, 4)]
    targets += [k.on_first(d) for d in range(1, 8)] + [k.on_second(d) for d in range(1, 8)]
    for target in targets:
        pl.semaphore_signal(barrier, inc=1, device_id=target, device_id_type=MESH)
    g.greet(barrier)
    loads = [
        pltpu.make_async_copy(src, dst, lsem.at[i])
        for i, (src, dst) in enumerate(((tok_hbm, tok_ref), (cot_hbm, cot_ref), (w_hbm, w_ref)))
    ]
    for load in loads:
        load.start()
    g.meet(barrier, len(targets))

    def copy(src, dst, slot, target):
        return remote(src, dst, tsem, usem, slot, target)

    outer_before = both(g.has_outer, g.has_before)
    outer_after = both(g.has_outer, g.has_after)
    outer_down = copy(terms.at[2 * core], youter.at[0], 0, g.before)
    outer_up = copy(terms.at[6 + 2 * core], youter.at[1], 1, g.after)
    groups[0].start_core()
    pl.when(outer_before)(outer_down.start)
    pl.when(outer_after)(outer_up.start)
    groups[1].start_core()
    to_partner = {}
    for a in (0, 2, 1):
        to_partner[a] = copy(terms.at[3 * a + 2 * (1 - core)], part.at[a], 2 + a, g.partner)
        to_partner[a].start()
    for load in loads:
        load.wait()
    grad_normed[...] = dot_general(gq_ref[...], w_ref[:, :width], 1, 1)
    for group in groups:
        group.start_scatter()

    to_partner[0].wait()
    sums[0] = (terms[1].astype(F32) + part[0].astype(F32)).astype(BF16)
    down = copy(sums.at[0], ysum.at[0], 5, g.before)
    pl.when(g.has_before)(down.start)
    to_partner[2].wait()
    sums[1] = (terms[7].astype(F32) + part[2].astype(F32)).astype(BF16)
    up = copy(sums.at[1], ysum.at[1], 6, g.after)
    pl.when(g.has_after)(up.start)
    to_partner[1].wait()
    for group in groups:
        group.start_second()

    outward = copy(osum, xin, 7, g.outer)

    @pl.when(g.has_outer)
    def _():
        acc[...] = terms[3 + 2 * core].astype(F32)

        @pl.when(g.has_after)
        def _():
            outer_down.wait_recv()
            acc[...] += youter[0].astype(F32)

        @pl.when(g.has_before)
        def _():
            outer_up.wait_recv()
            acc[...] += youter[1].astype(F32)

        osum[...] = acc[...].astype(BF16)
        outward.start()

    for group in groups:
        group.start_x()
    for group in groups:
        group.start_gather()
    acc[...] = terms[4].astype(F32) + part[1].astype(F32)

    @pl.when(g.has_after)
    def _():
        down.wait_recv()
        acc[...] += ysum[0].astype(F32)

    @pl.when(g.has_before)
    def _():
        up.wait_recv()
        acc[...] += ysum[1].astype(F32)

    @pl.when(g.has_outer)
    def _():
        outward.wait()
        acc[...] += xin[...].astype(F32)

    gkv[...] = acc[...].astype(BF16)
    gain = gain_ref[...].reshape(1, -1)
    _, centred, inverse = norm_parts(tok_ref[...])
    scaled = (grad_normed[...] + dot_general(gkv[...], w_ref[:, width:], 1, 1)) * gain
    inner = inverse * (
        scaled
        - jnp.mean(scaled, -1, keepdims=True)
        - centred * jnp.mean(scaled * centred, -1, keepdims=True)
    )
    gt_ref[...] = (cot_ref[...].astype(F32) + inner).astype(BF16)
    for group in groups:
        group.forward()
    products = jnp.zeros((width, 128), F32)
    for half, group in enumerate(groups):
        group.finish()
        for c in range(2 * n):
            place_at = half * 2 * n + c
            value = group.full[c * width:(c + 1) * width, :].astype(F32) * factor
            if place_at < 3 * n:
                lanes = slice(place_at * 128, (place_at + 1) * 128)
                oq_ref[:, lanes] = value
                products += value * w_ref[:, lanes].astype(F32)
            else:
                oo_ref[:, (place_at - 3 * n) * 128:(place_at - 3 * n + 1) * 128] = value
    total = jnp.broadcast_to(jnp.sum(products, -1, keepdims=True), (width, 128)).T
    og_ref[...] = total[:8, :] / gain
    pl.when(outer_before)(outer_down.wait_send)
    pl.when(outer_after)(outer_up.wait_send)
    pl.when(g.has_before)(down.wait_send)
    pl.when(g.has_after)(up.wait_send)


def reduce(factor, tokens, cotangent, gain, weight, grad_q, terms, mine):
    count, width = tokens.shape
    tile = (count, 2 * width)

    def body(*refs):
        reduce_kernel(factor, *refs)

    return pl.pallas_call(
        body,
        out_shape=(
            jax.ShapeDtypeStruct((count, width), BF16),
            jax.ShapeDtypeStruct((width, 3 * width), F32),
            jax.ShapeDtypeStruct((width, width), F32),
            jax.ShapeDtypeStruct((8, width), F32),
        ),
        in_specs=[HBM, HBM, VMEM, HBM] + [VMEM] * 3,
        out_specs=(VMEM,) * 4,
        scratch_shapes=[
            pltpu.VMEM((3,) + tile, BF16),
            pltpu.VMEM((2,) + tile, BF16),
            pltpu.VMEM((2,) + tile, BF16),
            pltpu.VMEM((2,) + tile, BF16),
            pltpu.VMEM(tile, BF16),
            pltpu.VMEM(tile, BF16),
            pltpu.VMEM(tile, F32),
            pltpu.VMEM(tile, BF16),
            pltpu.VMEM((count, width), F32),
            pltpu.VMEM((count, width), BF16),
            pltpu.VMEM((count, width), BF16),
            pltpu.VMEM((width, 3 * width), BF16),
            pltpu.SemaphoreType.DMA((3,)),
            pltpu.SemaphoreType.DMA((8,)),
            pltpu.SemaphoreType.DMA((8,)),
        ] + Reduction.scratch(UNIT) * 2,
        compiler_params=pltpu.CompilerParams(
            collective_id=0, has_side_effects=True, vmem_limit_bytes=LIMIT
        ),
        name="key_terms_and_all_reduce",
    )(tokens, cotangent, gain, weight, grad_q, terms, mine)


def on_device(tokens, cotangent, key_blocks, qkv_weight, out_weight, norm_gain):
    width = tokens.shape[-1]
    rows = tokens.reshape(-1, width)
    count = rows.shape[0]
    gain = pltpu.with_memory_space_constraint(norm_gain, pltpu.HBM)
    cot_rows = cotangent.reshape(-1, width)
    block_list = key_blocks.reshape(key_blocks.shape[2], key_blocks.shape[3])
    blocks = block_list.shape[0]
    rows, cot_rows, qkv_weight, out_weight = (
        pltpu.with_memory_space_constraint(a, pltpu.HBM)
        for a in (rows, cot_rows, qkv_weight, out_weight)
    )
    queries, grad_attended, neighbourhood, normed = project(
        rows, cot_rows, gain, qkv_weight, out_weight
    )
    grad_queries, key_terms, layer_rows, mine = attention(
        block_list, queries, grad_attended,
        neighbourhood.reshape(9 * blocks, count // blocks, 2 * width), normed,
        rows, cot_rows, out_weight,
    )
    factor = 1.0 / math.sqrt(count * lax.axis_size("tm") * lax.axis_size("height"))
    grad_tokens, grad_qkv, grad_out, grad_gain = reduce(
        factor, rows, cot_rows, gain, qkv_weight, grad_queries,
        key_terms.reshape(9, count, 2 * width), mine,
    )
    return (
        layer_rows.reshape(tokens.shape),
        grad_tokens.reshape(tokens.shape),
        grad_qkv,
        grad_out,
        grad_gain[0],
    )


def solution(mesh):
    split = P("tm", "height", None, None)
    return jax.shard_map(
        on_device, mesh=mesh,
        in_specs=(split, split, split, P(), P(), P()),
        out_specs=(split, split, P(), P(), P()),
        check_vma=False,
    )
```
